256 devices in a mesh: seq: 32 (over z, x_hi, core), chan: 8 (over y, x_lo).
Axes of the slice: x: 4 (x_hi: 2, x_lo: 2; x = x_hi * 2 + x_lo), y: 4, z: 8, core: 2. Of those that a mesh axis runs over, the one named last changes fastest.
Arguments:
- inputs: bfloat16 [131072, 2048], P('seq', 'chan'), may hold values from -6 to 6
- twiddle: float32 [256, 512], P('seq'), may hold values from -4 to 4
- right_factor: bfloat16 [512, 512], replicated, may hold values from -0.25 to 0.25
- left_factor: bfloat16 [256, 256], replicated, may hold values from -0.375 to 0.375
- blocks: bfloat16 [2048, 512], P('chan'), may hold values from -0.25 to 0.25
- block_mixer: float32 [512, 4, 4], replicated, may hold values from -3 to 3
- out_grad: bfloat16 [131072, 2048], P('seq', 'chan'), may hold values from -6 to 6
Outputs:
- output: bfloat16 [131072, 2048], P('seq', 'chan')
- input_grad: bfloat16 [131072, 2048], P('seq', 'chan')
The draws below stay inside these ranges and needn't reach their ends.
All inputs are finite; a program needn't handle non-finite values.
Results may differ from the reference program's by a relative error of at most 0.0076.
Values may be sent and summed in bfloat16 or wider, within the bound.
No kernel may reach another device: no remote copies, remote signals or barrier semaphores. Data moves between devices by JAX's collectives and lax.ppermute only.
A program may use at most 128 MiB of HBM per device.

```python
import jax
import jax.numpy as jnp
from jax import lax

SA = 256
SB = 512
D = 2048
BW = 512
NBLK = 4
SEQ_LEN = 131072


def block_levels(own_key, dims, cuts, low, high):
    level, own = 1.0, jax.random.fold_in(own_key, 6)
    for axis_at, shards_of in cuts:
        steps = jnp.exp(jax.random.uniform(jax.random.fold_in(own, axis_at), (shards_of,), jnp.float32, low / len(cuts), high / len(cuts)))
        level = level * jnp.repeat(steps, dims[axis_at] // shards_of).reshape([-1 if axis == axis_at else 1 for axis in range(len(dims))])
    return level


def scatter_about(rng, shape, scale, most, shards=(), held_as=jnp.bfloat16):
    result = jax.random.normal(rng, shape, jnp.float32) * scale
    if len(shards) > 0:
        result = block_levels(rng, shape, shards, -0.22, 0.18) * result
    return jnp.clip(result, min=-most, max=most).astype(held_as)


def setup_inputs(seed: int = 0) -> dict:
    splits = jax.random.split(jax.random.key(seed), 8)
    inputs = scatter_about(splits[0], (SEQ_LEN, D), 1.0, 6.0, ((0, 32), (1, 8)))
    twiddle = scatter_about(splits[1], (SA, SB), 1.0, 4.0, ((0, 32),), jnp.float32)
    right_factor = scatter_about(splits[2], (SB, SB), SB ** -0.5, 0.25)
    left_factor = scatter_about(splits[3], (SA, SA), SA ** -0.5, 0.375)
    blocks = scatter_about(splits[4], (D, BW), BW ** -0.5, 0.25, ((0, 8),))
    block_mixer = scatter_about(splits[5], (BW, NBLK, NBLK), NBLK ** -0.5, 3.0, (), jnp.float32)
    out_grad = scatter_about(splits[6], (SEQ_LEN, D), 1.0, 6.0, ((0, 32), (1, 8)))
    return dict(inputs=inputs, twiddle=twiddle, right_factor=right_factor, left_factor=left_factor, blocks=blocks, block_mixer=block_mixer, out_grad=out_grad)


def reference(inputs, twiddle, right_factor, left_factor, blocks, block_mixer, out_grad):
    group_size = min(D, 256)
    group_count = D // group_size
    right_wide = right_factor.astype(jnp.float32)
    left_wide = left_factor.astype(jnp.float32)

    def to_groups(array):
        return array.reshape(SA, SB, group_count, group_size).transpose(2, 0, 1, 3)

    def from_groups(array):
        return array.transpose(1, 2, 0, 3).reshape(SA * SB, D)

    def forward_seq(values):
        first_section = jnp.einsum('jb,abc->ajc', right_wide, values.astype(jnp.float32))
        twisted = (first_section * twiddle[:, :, None]).astype(jnp.bfloat16)
        return jnp.einsum('ia,ajc->ijc', left_wide, twisted.astype(jnp.float32)).astype(jnp.bfloat16)

    mixed = from_groups(lax.map(forward_seq, to_groups(inputs)))
    block_table = blocks.reshape(NBLK, BW, BW).astype(jnp.float32)

    def channel_row(pieces):
        x_row, mixed_row, grad_row = pieces
        split = x_row.reshape(SB, NBLK, BW).astype(jnp.float32)
        middle = jnp.einsum('bpq,pkq->bpk', split, block_table).astype(jnp.bfloat16)
        gate = jnp.einsum('bpk,kop->bok', middle.astype(jnp.float32), block_mixer,
                          precision=lax.Precision.HIGHEST).reshape(SB, D).astype(jnp.bfloat16)
        output_row = (gate.astype(jnp.float32) * mixed_row.astype(jnp.float32)).astype(jnp.bfloat16)
        grad_gate = (grad_row.astype(jnp.float32) * mixed_row.astype(jnp.float32)).astype(jnp.bfloat16)
        grad_mixed = (grad_row.astype(jnp.float32) * gate.astype(jnp.float32)).astype(jnp.bfloat16)
        grad_middle = jnp.einsum('bok,kop->bpk', grad_gate.reshape(SB, NBLK, BW).astype(jnp.float32),
                                 block_mixer, precision=lax.Precision.HIGHEST).astype(jnp.bfloat16)
        chan_grad = jnp.einsum('bpk,pkq->bpq', grad_middle.astype(jnp.float32),
                               block_table).reshape(SB, D).astype(jnp.bfloat16)
        return output_row, chan_grad, grad_mixed

    output, chan_grad, grad_mixed = lax.map(
        channel_row, (inputs.reshape(SA, SB, D), mixed.reshape(SA, SB, D), out_grad.reshape(SA, SB, D)))

    def backward_seq(values):
        grad_twisted = jnp.einsum('ia,ijc->ajc', left_wide, values.astype(jnp.float32)).astype(jnp.bfloat16)
        grad_first = (grad_twisted.astype(jnp.float32) * twiddle[:, :, None]).astype(jnp.bfloat16)
        return jnp.einsum('jb,ajc->abc', right_wide, grad_first.astype(jnp.float32))

    seq_grad = from_groups(lax.map(backward_seq, to_groups(grad_mixed.reshape(SA * SB, D))))
    input_grad = (seq_grad + chan_grad.reshape(SA * SB, D).astype(jnp.float32)).astype(jnp.bfloat16)
    return output.reshape(SA * SB, D), input_grad
```

```python
import jax
import jax.numpy as jnp
from jax import lax
from jax.experimental import pallas as pl
from jax.experimental.pallas import tpu as pltpu
from jax.sharding import PartitionSpec as P


F32 = jnp.float32
BF16 = jnp.bfloat16
NY = 4


def _params(mib=48):
    return pltpu.CompilerParams(vmem_limit_bytes=min(mib << 20, 67043328))


def _hbm(shape):
    return pltpu.HBM(shape, BF16)


def _cost(flops, nbytes):
    return pl.CostEstimate(flops=flops, bytes_accessed=nbytes, transcendentals=0)


def _fwd(s, d):
    return lax.rem(s[0] // 2 + d, NY)


def _back(s, d):
    return lax.rem(s[0] // 2 + NY - d, NY)


def _column(row, length):
    return jnp.transpose(jnp.broadcast_to(row, (128, length)))


def right_kernel(x_ref, r_ref, tw_ref, out_ref, scr):
    outer, _, chan = x_ref.shape
    rows = r_ref.shape[0]
    for a in range(outer):
        acc = jnp.dot(r_ref[...], x_ref[a], preferred_element_type=F32)
        col = _column(tw_ref[a : a + 1, :], rows)
        for c in range(chan // 128):
            scr[c, pl.ds(a, rows, stride=outer), :] = acc[:, c * 128 : c * 128 + 128] * col
    for c in range(chan // 128):
        out_ref[:, :, :, c * 128 : c * 128 + 128] = scr[c].reshape(*out_ref.shape[:3], 128).astype(BF16)


def right_pass(x3, right, twiddle, seq):
    outer, inner, chan = x3.shape
    steps = 2
    rows = inner // steps
    per = inner // seq
    return pl.pallas_call(
        right_kernel,
        name="right_pass",
        grid=(steps,),
        in_specs=[
            pl.BlockSpec((outer, inner, chan), lambda g: (0, 0, 0)),
            pl.BlockSpec((rows, inner), lambda g: (g, 0)),
            pl.BlockSpec((outer, rows), lambda g: (0, g)),
        ],
        out_specs=pl.BlockSpec((seq // steps, per, outer, chan), lambda g: (g, 0, 0, 0)),
        out_shape=_hbm((seq, per, outer, chan)),
        scratch_shapes=[pltpu.VMEM((chan // 128, rows * outer, 128), F32)],
        compiler_params=_params(64),
        cost_estimate=_cost(2 * outer * inner * inner * chan, 6 << 20),
    )(x3, right, twiddle)


def left_kernel(l_ref, in_ref, out_ref):
    seq, per, outer, chan = in_ref.shape
    for j in range(per):
        block = in_ref[:, j].astype(F32).reshape(seq * outer, chan).astype(BF16)
        acc = jnp.dot(l_ref[...], block, preferred_element_type=F32)
        out_ref[:, j] = acc.reshape(seq, outer, chan).astype(BF16)


def left_pass(left, wire):
    seq, per, outer, chan = wire.shape
    steps = 4
    full = seq * outer
    block = (seq, per // steps, outer, chan)
    return pl.pallas_call(
        left_kernel,
        name="left_pass",
        grid=(steps,),
        in_specs=[
            pl.BlockSpec((full, full), lambda g: (0, 0)),
            pl.BlockSpec(block, lambda g: (0, g, 0, 0)),
        ],
        out_specs=pl.BlockSpec(block, lambda g: (0, g, 0, 0)),
        out_shape=_hbm(wire.shape),
        compiler_params=_params(),
        cost_estimate=_cost(2 * full * full * per * chan, 4 << 20),
    )(left, wire)


def middle_kernel(s, x_ref, xr_ref, b_ref, bo_ref, *outs):
    d = pl.program_id(0)
    half_outer, rows, chan = x_ref.shape
    half = lax.rem(s[0], 2)
    own = pl.ds(pl.multiple_of(half * chan, 128), chan)
    other = pl.ds(pl.multiple_of((1 - half) * chan, 128), chan)
    dims = (((1,), (1,)), ((), ()))
    x = x_ref[...].reshape(half_outer * rows, chan)
    xr = xr_ref[...].reshape(half_outer * rows, chan)
    values = []
    for ref in (b_ref, bo_ref):
        acc = lax.dot_general(x, ref[:, own], dims, preferred_element_type=F32)
        acc += lax.dot_general(xr, ref[:, other], dims, preferred_element_type=F32)
        values.append(acc.astype(BF16))
    for i in range(NY):

        @pl.when(d == i)
        def _():
            outs[i][0] = values[0]
            outs[i][1] = values[1]


def middle_pass(s, x3, xr, blocks, blocks_other):
    half_outer, inner, chan = xr.shape
    rows = inner // NY
    block = (half_outer, rows, chan)
    part = (2, half_outer * rows, chan)
    whole = pl.BlockSpec(blocks.shape, lambda d, s: (0, 0))
    return pl.pallas_call(
        middle_kernel,
        name="middle_pass",
        grid_spec=pltpu.PrefetchScalarGridSpec(
            num_scalar_prefetch=1,
            grid=(NY,),
            in_specs=[
                pl.BlockSpec(block, lambda d, s: (lax.rem(s[0], 2), _fwd(s, d), 0)),
                pl.BlockSpec(block, lambda d, s: (0, _fwd(s, d), 0)),
                whole,
                whole,
            ],
            out_specs=[pl.BlockSpec(part, lambda d, s: (0, 0, 0))] * NY,
        ),
        out_shape=[jax.ShapeDtypeStruct(part, BF16)] * NY,
        compiler_params=_params(),
        cost_estimate=_cost(8 * half_outer * inner * chan * chan, 5 << 20),
    )(s, x3, xr, blocks, blocks_other)


def _mixed(s, mix_ref, values, e, k, flip):
    y = s[0] // 2
    chan = values[0].shape[-1]
    cols = pl.ds(pl.multiple_of(lax.rem(s[0] + k, 2) * chan, 128), chan)
    to = lax.rem(y + e, NY)
    acc = None
    for d in range(NY):
        frm = lax.rem(y + NY - d, NY)
        row = mix_ref[frm, pl.ds(to, 1), cols] if flip else mix_ref[to, pl.ds(frm, 1), cols]
        term = values[d] * row
        acc = term if acc is None else acc + term
    return acc.astype(BF16)


def mix_kernel(s, mix_ref, *refs):
    ins, outs = refs[:NY], refs[NY:]
    for k in range(2):
        values = [r[k].astype(F32) for r in ins]
        for e in range(NY):
            outs[2 * e + k][...] = _mixed(s, mix_ref, values, e, k, False)


def mix_pass(s, mixer, parts):
    _, total, chan = parts[0].shape
    steps = 2
    out_block = pl.BlockSpec((total // steps, chan), lambda g, s: (g, 0))
    return pl.pallas_call(
        mix_kernel,
        name="mix_pass",
        grid_spec=pltpu.PrefetchScalarGridSpec(
            num_scalar_prefetch=1,
            grid=(steps,),
            in_specs=[pl.BlockSpec(mixer.shape, lambda g, s: (0, 0, 0))]
            + [pl.BlockSpec((2, total // steps, chan), lambda g, s: (0, g, 0))] * NY,
            out_specs=[out_block] * (2 * NY),
        ),
        out_shape=[jax.ShapeDtypeStruct((total, chan), BF16)] * (2 * NY),
        compiler_params=_params(),
        cost_estimate=_cost(4 * NY * NY * total * chan, 4 << 20),
    )(s, mixer, *parts)


def mix_back_kernel(s, mix_ref, *refs):
    ins, outs = refs[: 2 * NY], refs[2 * NY :]
    for k in range(2):
        values = [ins[2 * d + k][...].astype(F32) for d in range(NY)]
        for e in range(NY):
            outs[e][k] = _mixed(s, mix_ref, values, e, k, True)


def mix_back(s, mixer, pieces):
    total, chan = pieces[0].shape
    steps = 2
    in_block = pl.BlockSpec((total // steps, chan), lambda g, s: (g, 0))
    return pl.pallas_call(
        mix_back_kernel,
        name="mix_back",
        grid_spec=pltpu.PrefetchScalarGridSpec(
            num_scalar_prefetch=1,
            grid=(steps,),
            in_specs=[pl.BlockSpec(mixer.shape, lambda g, s: (0, 0, 0))] + [in_block] * (2 * NY),
            out_specs=[pl.BlockSpec((2, total // steps, chan), lambda g, s: (0, g, 0))] * NY,
        ),
        out_shape=[jax.ShapeDtypeStruct((2, total, chan), BF16)] * NY,
        compiler_params=_params(),
        cost_estimate=_cost(4 * NY * NY * total * chan, 4 << 20),
    )(s, mixer, *pieces)


def gate_kernel(s, og_ref, *refs):
    pieces, (gate_ref, wire_ref, scr) = refs[: 2 * NY], refs[2 * NY :]
    d = pl.program_id(0)
    outer, rows, chan = og_ref.shape
    for i in range(NY):

        @pl.when(d == i)
        def _():
            for k in range(2):
                start = lax.rem(s[0] + k, 2) * (outer // 2)
                gate_ref[pl.ds(start, outer // 2)] = pieces[2 * i + k][...].reshape(outer // 2, rows, chan)

    for a in range(outer):
        for c in range(chan // 128):
            cols = slice(c * 128, c * 128 + 128)
            scr[c, pl.ds(a, rows, stride=outer), :] = og_ref[a, :, cols].astype(F32) * gate_ref[a, :, cols].astype(F32)
    for c in range(chan // 128):
        wire_ref[:, :, :, c * 128 : c * 128 + 128] = scr[c].reshape(*wire_ref.shape[:3], 128).astype(BF16)


def gate_pass(s, og3, pieces, seq):
    outer, inner, chan = og3.shape
    rows = inner // NY
    per = inner // seq
    nat = pl.BlockSpec((outer, rows, chan), lambda d, s: (0, _back(s, d), 0))
    return pl.pallas_call(
        gate_kernel,
        name="gate_pass",
        grid_spec=pltpu.PrefetchScalarGridSpec(
            num_scalar_prefetch=1,
            grid=(NY,),
            in_specs=[nat] + [pl.BlockSpec(pieces[0].shape, lambda d, s: (0, 0))] * (2 * NY),
            out_specs=[nat, pl.BlockSpec((seq // NY, per, outer, chan), lambda d, s: (_back(s, d), 0, 0, 0))],
            scratch_shapes=[pltpu.VMEM((chan // 128, rows * outer, 128), F32)],
        ),
        out_shape=[
            jax.ShapeDtypeStruct(og3.shape, BF16),
            jax.ShapeDtypeStruct((seq, per, outer, chan), BF16),
        ],
        compiler_params=_params(),
        cost_estimate=_cost(outer * inner * chan, 8 << 20),
    )(s, og3, *pieces)


def out_kernel(s, wire_ref, gate_ref, og_ref, out_ref, *refs):
    pieces, (scr, tmp) = refs[: 2 * NY], refs[2 * NY :]
    d = pl.program_id(0)
    outer, rows, chan = og_ref.shape
    for c in range(chan // 128):
        scr[c] = wire_ref[:, :, :, c * 128 : c * 128 + 128].astype(F32).reshape(scr.shape[1:])
    for a in range(outer):
        for c in range(chan // 128):
            cols = slice(c * 128, c * 128 + 128)
            m = scr[c, pl.ds(a, rows, stride=outer), :]
            out_ref[a, :, cols] = (gate_ref[a, :, cols].astype(F32) * m).astype(BF16)
            tmp[a, :, cols] = (og_ref[a, :, cols].astype(F32) * m).astype(BF16)
    for i in range(NY):

        @pl.when(d == i)
        def _():
            for k in range(2):
                start = lax.rem(s[0] + k, 2) * (outer // 2)
                pieces[2 * i + k][...] = tmp[pl.ds(start, outer // 2)].reshape(pieces[0].shape)


def out_pass(s, wire, gate3, og3):
    outer, inner, chan = og3.shape
    seq, per = wire.shape[:2]
    rows = inner // NY
    piece = (outer // 2 * rows, chan)
    nat = pl.BlockSpec((outer, rows, chan), lambda d, s: (0, _fwd(s, d), 0))
    res = pl.pallas_call(
        out_kernel,
        name="out_pass",
        grid_spec=pltpu.PrefetchScalarGridSpec(
            num_scalar_prefetch=1,
            grid=(NY,),
            in_specs=[pl.BlockSpec((seq // NY, per, outer, chan), lambda d, s: (_fwd(s, d), 0, 0, 0)), nat, nat],
            out_specs=[nat] + [pl.BlockSpec(piece, lambda d, s: (0, 0))] * (2 * NY),
            scratch_shapes=[
                pltpu.VMEM((chan // 128, rows * outer, 128), F32),
                pltpu.VMEM((outer, rows, chan), BF16),
            ],
        ),
        out_shape=[jax.ShapeDtypeStruct(og3.shape, BF16)] + [jax.ShapeDtypeStruct(piece, BF16)] * (2 * NY),
        compiler_params=_params(),
        cost_estimate=_cost(2 * outer * inner * chan, 10 << 20),
    )(s, wire, gate3, og3)
    return res[0], res[1:]


def chan_kernel(s, b_ref, bo_ref, *refs):
    parts, (own_ref, other_ref) = refs[:NY], refs[NY:]
    d = pl.program_id(0)
    _, _, chan = own_ref.shape
    for i in range(NY):

        @pl.when(d == i)
        def _():
            for k, ref in enumerate((own_ref, other_ref)):
                cols = pl.ds(pl.multiple_of(lax.rem(s[0] + k, 2) * chan, 128), chan)
                acc = jnp.dot(parts[i][0], b_ref[:, cols], preferred_element_type=F32)
                acc += jnp.dot(parts[i][1], bo_ref[:, cols], preferred_element_type=F32)
                ref[...] = acc.astype(BF16).reshape(ref.shape)


def chan_pass(s, blocks, blocks_other, parts, half_outer):
    _, total, chan = parts[0].shape
    rows = total // half_outer
    whole = pl.BlockSpec(blocks.shape, lambda d, s: (0, 0))
    out = pl.BlockSpec((half_outer, rows, chan), lambda d, s: (0, _back(s, d), 0))
    return pl.pallas_call(
        chan_kernel,
        name="chan_pass",
        grid_spec=pltpu.PrefetchScalarGridSpec(
            num_scalar_prefetch=1,
            grid=(NY,),
            in_specs=[whole, whole] + [pl.BlockSpec(parts[0].shape, lambda d, s: (0, 0, 0))] * NY,
            out_specs=[out, out],
        ),
        out_shape=[jax.ShapeDtypeStruct((half_outer, rows * NY, chan), BF16)] * 2,
        compiler_params=_params(),
        cost_estimate=_cost(8 * total * NY * chan * chan, 5 << 20),
    )(s, blocks, blocks_other, *parts)


def tail_kernel(s, wire_ref, rt_ref, tw_ref, own_ref, other_ref, out_ref, scr):
    outer, inner = tw_ref.shape
    chan = out_ref.shape[2]
    a = pl.program_id(0)

    @pl.when(a == 0)
    def _():
        for c in range(chan // 128):
            scr[c] = wire_ref[:, :, :, c * 128 : c * 128 + 128].astype(F32).reshape(scr.shape[1:])

    col = _column(tw_ref[pl.ds(a, 1), :], inner)
    parts = []
    for c in range(chan // 128):
        parts.append((scr[c, pl.ds(a, inner, stride=outer), :] * col).astype(BF16))
    acc = jnp.dot(rt_ref[...], jnp.concatenate(parts, axis=1), preferred_element_type=F32)
    mine = a // (outer // 2) == lax.rem(s[0], 2)

    @pl.when(mine)
    def _():
        out_ref[0] = (acc + own_ref[0].astype(F32)).astype(BF16)

    @pl.when(jnp.logical_not(mine))
    def _():
        out_ref[0] = (acc + other_ref[0].astype(F32)).astype(BF16)


def tail_pass(s, wire, right_t, twiddle, own, other):
    half_outer, inner, chan = own.shape
    outer = 2 * half_outer

    def part(k):
        return lambda a, s: (jnp.clip(a - lax.rem(s[0] + k, 2) * half_outer, 0, half_outer - 1), 0, 0)

    return pl.pallas_call(
        tail_kernel,
        name="tail_pass",
        grid_spec=pltpu.PrefetchScalarGridSpec(
            num_scalar_prefetch=1,
            grid=(outer,),
            in_specs=[
                pl.BlockSpec(wire.shape, lambda a, s: (0, 0, 0, 0)),
                pl.BlockSpec(right_t.shape, lambda a, s: (0, 0)),
                pl.BlockSpec(twiddle.shape, lambda a, s: (0, 0)),
                pl.BlockSpec((1, inner, chan), part(0)),
                pl.BlockSpec((1, inner, chan), part(1)),
            ],
            out_specs=pl.BlockSpec((1, inner, chan), lambda a, s: (a, 0, 0)),
            scratch_shapes=[pltpu.VMEM((chan // 128, outer * inner, 128), F32)],
        ),
        out_shape=jax.ShapeDtypeStruct((outer, inner, chan), BF16),
        compiler_params=_params(),
        cost_estimate=_cost(2 * outer * inner * inner * chan, 7 << 20),
    )(s, wire, right_t, twiddle, own, other)


def seq_swap(wire):
    return lax.all_to_all(wire, "seq", split_axis=0, concat_axis=0, tiled=True)


def body(inputs, twiddle, right_factor, left_factor, blocks, block_mixer, out_grad):
    outer, inner = twiddle.shape
    chan = inputs.shape[1]
    seq = left_factor.shape[0] // outer
    n = 2 * NY

    def send(v, d, k):
        if d == 0 and k == 0:
            return v
        return lax.ppermute(v, "chan", [(c, (((c // 2 + d) % NY) * 2 + c % 2) ^ k) for c in range(n)])

    def around(parts):
        return [send(parts[d], d, 0) for d in range(NY)]

    def across(pieces):
        return [send(p, i // 2, i % 2) for i, p in enumerate(pieces)]

    s = lax.axis_index("chan").reshape(1)
    x3 = inputs.reshape(outer, inner, chan)
    og3 = out_grad.reshape(outer, inner, chan)
    mixer = jnp.transpose(block_mixer, (1, 2, 0))

    half = lax.rem(lax.axis_index("chan"), 2)
    xs = lax.dynamic_slice_in_dim(x3, (1 - half) * (outer // 2), outer // 2, 0)
    xr = send(xs, 0, 1)
    blocks_other = send(blocks, 0, 1)
    twisted = seq_swap(right_pass(x3, right_factor, twiddle, seq))
    middle = middle_pass(s, x3, xr, blocks, blocks_other)
    twisted, _ = lax.optimization_barrier((twisted, middle[0]))
    mixed_wire = left_pass(left_factor, twisted)

    middle = around(middle)
    *middle, _ = lax.optimization_barrier((*middle, mixed_wire))
    mixed = seq_swap(mixed_wire)
    pieces = mix_pass(s, mixer, middle)
    pieces = across(pieces)
    gate3, grad_mixed = gate_pass(s, og3, pieces, seq)

    grad_mixed, mixed = lax.optimization_barrier((grad_mixed, mixed))
    grad_wire = seq_swap(grad_mixed)
    output, pieces = out_pass(s, mixed, gate3, og3)
    pieces = across(pieces)
    grad_middle = mix_back(s, mixer, pieces)
    grad_wire, _ = lax.optimization_barrier((grad_wire, grad_middle[0]))
    grad_wire = left_pass(left_factor.T, grad_wire)

    grad_middle = around(grad_middle)
    grad_twisted = seq_swap(grad_wire)
    own, other = chan_pass(s, blocks, blocks_other, grad_middle, outer // 2)
    other = send(other, 0, 1)
    input_grad = tail_pass(s, grad_twisted, right_factor.T, twiddle, own, other)
    return (output.reshape(inputs.shape), input_grad.reshape(inputs.shape))


def solution(mesh):
    return jax.shard_map(
        body,
        mesh=mesh,
        in_specs=(
            P("seq", "chan"),
            P("seq", None),
            P(),
            P(),
            P("chan", None),
            P(),
            P("seq", "chan"),
        ),
        out_specs=(P("seq", "chan"), P("seq", "chan")),
        check_vma=False,
    )
```

```python
import jax
import jax.numpy as jnp
from jax import lax
from jax.experimental import pallas as pl
from jax.experimental.pallas import tpu as pltpu
from jax.sharding import PartitionSpec as P


F32 = jnp.float32
BF16 = jnp.bfloat16
NY = 4


def _params(mib=32):
    return pltpu.CompilerParams(vmem_limit_bytes=min(mib << 20, 67043328))


def _hbm(shape):
    return pltpu.HBM(shape, BF16)


def _cost(flops, nbytes):
    return pl.CostEstimate(flops=flops, bytes_accessed=nbytes, transcendentals=0)


def _fwd(s, d):
    return lax.rem(s[0] // 2 + d, NY)


def _back(s, d):
    return lax.rem(s[0] // 2 + NY - d, NY)


def _column(row, length):
    return jnp.transpose(jnp.broadcast_to(row, (128, length)))


def right_kernel(x_ref, r_ref, tw_ref, out_ref, scr):
    outer, _, chan = x_ref.shape
    rows = r_ref.shape[0]
    for a in range(outer):
        acc = jnp.dot(r_ref[...], x_ref[a], preferred_element_type=F32)
        col = _column(tw_ref[a : a + 1, :], rows)
        for c in range(chan // 128):
            scr[c, pl.ds(a, rows, stride=outer), :] = acc[:, c * 128 : c * 128 + 128] * col
    for c in range(chan // 128):
        out_ref[:, :, :, c * 128 : c * 128 + 128] = scr[c].reshape(*out_ref.shape[:3], 128).astype(BF16)


def right_pass(x3, right, twiddle, seq):
    outer, inner, chan = x3.shape
    steps = 2
    rows = inner // steps
    per = inner // seq
    return pl.pallas_call(
        right_kernel,
        name="right_pass",
        grid=(steps,),
        in_specs=[
            pl.BlockSpec((outer, inner, chan), lambda g: (0, 0, 0)),
            pl.BlockSpec((rows, inner), lambda g: (g, 0)),
            pl.BlockSpec((outer, rows), lambda g: (0, g)),
        ],
        out_specs=pl.BlockSpec((seq // steps, per, outer, chan), lambda g: (g, 0, 0, 0)),
        out_shape=_hbm((seq, per, outer, chan)),
        scratch_shapes=[pltpu.VMEM((chan // 128, rows * outer, 128), F32)],
        compiler_params=_params(64),
        cost_estimate=_cost(2 * outer * inner * inner * chan, 6 << 20),
    )(x3, right, twiddle)


def left_kernel(l_ref, in_ref, out_ref):
    seq, per, outer, chan = in_ref.shape
    for j in range(per):
        block = in_ref[:, j].astype(F32).reshape(seq * outer, chan).astype(BF16)
        acc = jnp.dot(l_ref[...], block, preferred_element_type=F32)
        out_ref[:, j] = acc.reshape(seq, outer, chan).astype(BF16)


def left_pass(left, wire):
    seq, per, outer, chan = wire.shape
    steps = 4
    full = seq * outer
    block = (seq, per // steps, outer, chan)
    return pl.pallas_call(
        left_kernel,
        name="left_pass",
        grid=(steps,),
        in_specs=[
            pl.BlockSpec((full, full), lambda g: (0, 0)),
            pl.BlockSpec(block, lambda g: (0, g, 0, 0)),
        ],
        out_specs=pl.BlockSpec(block, lambda g: (0, g, 0, 0)),
        out_shape=_hbm(wire.shape),
        compiler_params=_params(),
        cost_estimate=_cost(2 * full * full * per * chan, 4 << 20),
    )(left, wire)


def middle_kernel(s, x_ref, xr_ref, b_ref, bo_ref, *outs):
    d = pl.program_id(0)
    half_outer, rows, chan = x_ref.shape
    half = lax.rem(s[0], 2)
    own = pl.ds(pl.multiple_of(half * chan, 128), chan)
    other = pl.ds(pl.multiple_of((1 - half) * chan, 128), chan)
    dims = (((1,), (1,)), ((), ()))
    x = x_ref[...].reshape(half_outer * rows, chan)
    xr = xr_ref[...].reshape(half_outer * rows, chan)
    values = []
    for ref in (b_ref, bo_ref):
        acc = lax.dot_general(x, ref[:, own], dims, preferred_element_type=F32)
        acc += lax.dot_general(xr, ref[:, other], dims, preferred_element_type=F32)
        values.append(acc.astype(BF16))
    for i in range(NY):

        @pl.when(d == i)
        def _():
            outs[i][0] = values[0]
            outs[i][1] = values[1]


def middle_pass(s, x3, xr, blocks, blocks_other):
    half_outer, inner, chan = xr.shape
    rows = inner // NY
    block = (half_outer, rows, chan)
    part = (2, half_outer * rows, chan)
    whole = pl.BlockSpec(blocks.shape, lambda d, s: (0, 0))
    return pl.pallas_call(
        middle_kernel,
        name="middle_pass",
        grid_spec=pltpu.PrefetchScalarGridSpec(
            num_scalar_prefetch=1,
            grid=(NY,),
            in_specs=[
                pl.BlockSpec(block, lambda d, s: (lax.rem(s[0], 2), _fwd(s, d), 0)),
                pl.BlockSpec(block, lambda d, s: (0, _fwd(s, d), 0)),
                whole,
                whole,
            ],
            out_specs=[pl.BlockSpec(part, lambda d, s: (0, 0, 0))] * NY,
        ),
        out_shape=[_hbm(part)] * NY,
        compiler_params=_params(),
        cost_estimate=_cost(8 * half_outer * inner * chan * chan, 5 << 20),
    )(s, x3, xr, blocks, blocks_other)


def _mixed(s, mix_ref, values, e, k, flip):
    y = s[0] // 2
    chan = values[0].shape[-1]
    cols = pl.ds(pl.multiple_of(lax.rem(s[0] + k, 2) * chan, 128), chan)
    to = lax.rem(y + e, NY)
    acc = None
    for d in range(NY):
        frm = lax.rem(y + NY - d, NY)
        row = mix_ref[frm, pl.ds(to, 1), cols] if flip else mix_ref[to, pl.ds(frm, 1), cols]
        term = values[d] * row
        acc = term if acc is None else acc + term
    return acc.astype(BF16)


def mix_kernel(s, mix_ref, *refs):
    ins, outs = refs[:NY], refs[NY:]
    for k in range(2):
        values = [r[k].astype(F32) for r in ins]
        for e in range(NY):
            outs[2 * e + k][...] = _mixed(s, mix_ref, values, e, k, False)


def mix_pass(s, mixer, parts):
    _, total, chan = parts[0].shape
    steps = 2
    out_block = pl.BlockSpec((total // steps, chan), lambda g, s: (g, 0))
    return pl.pallas_call(
        mix_kernel,
        name="mix_pass",
        grid_spec=pltpu.PrefetchScalarGridSpec(
            num_scalar_prefetch=1,
            grid=(steps,),
            in_specs=[pl.BlockSpec(mixer.shape, lambda g, s: (0, 0, 0))]
            + [pl.BlockSpec((2, total // steps, chan), lambda g, s: (0, g, 0))] * NY,
            out_specs=[out_block] * (2 * NY),
        ),
        out_shape=[_hbm((total, chan))] * (2 * NY),
        compiler_params=_params(),
        cost_estimate=_cost(4 * NY * NY * total * chan, 4 << 20),
    )(s, mixer, *parts)


def mix_back_kernel(s, mix_ref, *refs):
    ins, outs = refs[: 2 * NY], refs[2 * NY :]
    for k in range(2):
        values = [ins[2 * d + k][...].astype(F32) for d in range(NY)]
        for e in range(NY):
            outs[e][k] = _mixed(s, mix_ref, values, e, k, True)


def mix_back(s, mixer, pieces):
    total, chan = pieces[0].shape
    steps = 2
    in_block = pl.BlockSpec((total // steps, chan), lambda g, s: (g, 0))
    return pl.pallas_call(
        mix_back_kernel,
        name="mix_back",
        grid_spec=pltpu.PrefetchScalarGridSpec(
            num_scalar_prefetch=1,
            grid=(steps,),
            in_specs=[pl.BlockSpec(mixer.shape, lambda g, s: (0, 0, 0))] + [in_block] * (2 * NY),
            out_specs=[pl.BlockSpec((2, total // steps, chan), lambda g, s: (0, g, 0))] * NY,
        ),
        out_shape=[_hbm((2, total, chan))] * NY,
        compiler_params=_params(),
        cost_estimate=_cost(4 * NY * NY * total * chan, 4 << 20),
    )(s, mixer, *pieces)


def gate_kernel(s, og_ref, *refs):
    pieces, (gate_ref, wire_ref, scr) = refs[: 2 * NY], refs[2 * NY :]
    d = pl.program_id(0)
    outer, rows, chan = og_ref.shape
    for i in range(NY):

        @pl.when(d == i)
        def _():
            for k in range(2):
                start = lax.rem(s[0] + k, 2) * (outer // 2)
                gate_ref[pl.ds(start, outer // 2)] = pieces[2 * i + k][...].reshape(outer // 2, rows, chan)

    for a in range(outer):
        for c in range(chan // 128):
            cols = slice(c * 128, c * 128 + 128)
            scr[c, pl.ds(a, rows, stride=outer), :] = og_ref[a, :, cols].astype(F32) * gate_ref[a, :, cols].astype(F32)
    for c in range(chan // 128):
        wire_ref[:, :, :, c * 128 : c * 128 + 128] = scr[c].reshape(*wire_ref.shape[:3], 128).astype(BF16)


def gate_pass(s, og3, pieces, seq):
    outer, inner, chan = og3.shape
    rows = inner // NY
    per = inner // seq
    nat = pl.BlockSpec((outer, rows, chan), lambda d, s: (0, _back(s, d), 0))
    return pl.pallas_call(
        gate_kernel,
        name="gate_pass",
        grid_spec=pltpu.PrefetchScalarGridSpec(
            num_scalar_prefetch=1,
            grid=(NY,),
            in_specs=[nat] + [pl.BlockSpec(pieces[0].shape, lambda d, s: (0, 0))] * (2 * NY),
            out_specs=[nat, pl.BlockSpec((seq // NY, per, outer, chan), lambda d, s: (_back(s, d), 0, 0, 0))],
            scratch_shapes=[pltpu.VMEM((chan // 128, rows * outer, 128), F32)],
        ),
        out_shape=[
            _hbm(og3.shape),
            _hbm((seq, per, outer, chan)),
        ],
        compiler_params=_params(),
        cost_estimate=_cost(outer * inner * chan, 8 << 20),
    )(s, og3, *pieces)


def out_kernel(s, wire_ref, gate_ref, og_ref, out_ref, *refs):
    pieces, (scr, tmp) = refs[: 2 * NY], refs[2 * NY :]
    d = pl.program_id(0)
    outer, rows, chan = og_ref.shape
    for c in range(chan // 128):
        scr[c] = wire_ref[:, :, :, c * 128 : c * 128 + 128].astype(F32).reshape(scr.shape[1:])
    for a in range(outer):
        for c in range(chan // 128):
            cols = slice(c * 128, c * 128 + 128)
            m = scr[c, pl.ds(a, rows, stride=outer), :]
            out_ref[a, :, cols] = (gate_ref[a, :, cols].astype(F32) * m).astype(BF16)
            tmp[a, :, cols] = (og_ref[a, :, cols].astype(F32) * m).astype(BF16)
    for i in range(NY):

        @pl.when(d == i)
        def _():
            for k in range(2):
                start = lax.rem(s[0] + k, 2) * (outer // 2)
                pieces[2 * i + k][...] = tmp[pl.ds(start, outer // 2)].reshape(pieces[0].shape)


def out_pass(s, wire, gate3, og3):
    outer, inner, chan = og3.shape
    seq, per = wire.shape[:2]
    rows = inner // NY
    piece = (outer // 2 * rows, chan)
    nat = pl.BlockSpec((outer, rows, chan), lambda d, s: (0, _fwd(s, d), 0))
    res = pl.pallas_call(
        out_kernel,
        name="out_pass",
        grid_spec=pltpu.PrefetchScalarGridSpec(
            num_scalar_prefetch=1,
            grid=(NY,),
            in_specs=[pl.BlockSpec((seq // NY, per, outer, chan), lambda d, s: (_fwd(s, d), 0, 0, 0)), nat, nat],
            out_specs=[nat] + [pl.BlockSpec(piece, lambda d, s: (0, 0))] * (2 * NY),
            scratch_shapes=[
                pltpu.VMEM((chan // 128, rows * outer, 128), F32),
                pltpu.VMEM((outer, rows, chan), BF16),
            ],
        ),
        out_shape=[_hbm(og3.shape)] + [_hbm(piece)] * (2 * NY),
        compiler_params=_params(),
        cost_estimate=_cost(2 * outer * inner * chan, 10 << 20),
    )(s, wire, gate3, og3)
    return res[0], res[1:]


def chan_kernel(s, b_ref, bo_ref, part_ref, own_ref, other_ref):
    chan = own_ref.shape[1]
    for k, ref in enumerate((own_ref, other_ref)):
        cols = pl.ds(pl.multiple_of(lax.rem(s[0] + k, 2) * chan, 128), chan)
        acc = jnp.dot(part_ref[0], b_ref[:, cols], preferred_element_type=F32)
        acc += jnp.dot(part_ref[1], bo_ref[:, cols], preferred_element_type=F32)
        ref[...] = acc.astype(BF16)


def chan_pass(s, blocks, blocks_other, part):
    _, total, chan = part.shape
    whole = pl.BlockSpec(blocks.shape, lambda i, s: (0, 0))
    out = pl.BlockSpec((total, chan), lambda i, s: (0, 0))
    return pl.pallas_call(
        chan_kernel,
        name="chan_pass",
        grid_spec=pltpu.PrefetchScalarGridSpec(
            num_scalar_prefetch=1,
            grid=(1,),
            in_specs=[whole, whole, pl.BlockSpec(part.shape, lambda i, s: (0, 0, 0))],
            out_specs=[out, out],
        ),
        out_shape=[_hbm((total, chan))] * 2,
        compiler_params=_params(),
        cost_estimate=_cost(8 * total * chan * chan, 2 << 20),
    )(s, blocks, blocks_other, part)


def tail_kernel(s, wire_ref, rt_ref, tw_ref, *refs):
    own, other, (out_ref, scr, total_ref) = refs[:NY], refs[NY : 2 * NY], refs[2 * NY :]
    outer, inner = tw_ref.shape
    chan = out_ref.shape[2]
    rows = inner // NY
    a = pl.program_id(0)

    @pl.when(a == 0)
    def _():
        for c in range(chan // 128):
            scr[c] = wire_ref[:, :, :, c * 128 : c * 128 + 128].astype(F32).reshape(scr.shape[1:])

    col = _column(tw_ref[pl.ds(a, 1), :], inner)
    parts = []
    for c in range(chan // 128):
        parts.append((scr[c, pl.ds(a, inner, stride=outer), :] * col).astype(BF16))
    total_ref[...] = jnp.dot(rt_ref[...], jnp.concatenate(parts, axis=1), preferred_element_type=F32)
    mine = a // (outer // 2) == lax.rem(s[0], 2)

    def finish(refs):
        for d in range(NY):
            at = pl.ds(pl.multiple_of(_back(s, d) * rows, rows), rows)
            out_ref[0, at, :] = (total_ref[at, :] + refs[d][...].astype(F32)).astype(BF16)

    pl.when(mine)(lambda: finish(own))
    pl.when(jnp.logical_not(mine))(lambda: finish(other))


def tail_pass(s, wire, right_t, twiddle, own, other):
    outer, inner = twiddle.shape
    chan = wire.shape[3]
    half_outer, rows = outer // 2, inner // NY

    def part(k):
        block = (rows, chan)
        return pl.BlockSpec(block, lambda a, s: (jnp.clip(a - lax.rem(s[0] + k, 2) * half_outer, 0, half_outer - 1), 0))

    return pl.pallas_call(
        tail_kernel,
        name="tail_pass",
        grid_spec=pltpu.PrefetchScalarGridSpec(
            num_scalar_prefetch=1,
            grid=(outer,),
            in_specs=[
                pl.BlockSpec(wire.shape, lambda a, s: (0, 0, 0, 0)),
                pl.BlockSpec(right_t.shape, lambda a, s: (0, 0)),
                pl.BlockSpec(twiddle.shape, lambda a, s: (0, 0)),
            ]
            + [part(0)] * NY
            + [part(1)] * NY,
            out_specs=pl.BlockSpec((1, inner, chan), lambda a, s: (a, 0, 0)),
            scratch_shapes=[pltpu.VMEM((chan // 128, outer * inner, 128), F32), pltpu.VMEM((inner, chan), F32)],
        ),
        out_shape=jax.ShapeDtypeStruct((outer, inner, chan), BF16),
        compiler_params=_params(64),
        cost_estimate=_cost(2 * outer * inner * inner * chan, 7 << 20),
    )(s, wire, right_t, twiddle, *own, *other)


def seq_swap(wire):
    return lax.all_to_all(wire, "seq", split_axis=0, concat_axis=0, tiled=True)


def body(inputs, twiddle, right_factor, left_factor, blocks, block_mixer, out_grad):
    outer, inner = twiddle.shape
    chan = inputs.shape[1]
    seq = left_factor.shape[0] // outer
    n = 2 * NY

    def send(v, d, k):
        if d == 0 and k == 0:
            return v
        return lax.ppermute(v, "chan", [(c, (((c // 2 + d) % NY) * 2 + c % 2) ^ k) for c in range(n)])

    def around(parts):
        return [send(parts[d], d, 0) for d in range(NY)]

    def across(pieces):
        return [send(p, i // 2, i % 2) for i, p in enumerate(pieces)]

    s = lax.axis_index("chan").reshape(1)
    x3 = inputs.reshape(outer, inner, chan)
    og3 = out_grad.reshape(outer, inner, chan)
    mixer = jnp.transpose(block_mixer, (1, 2, 0))

    half = lax.rem(lax.axis_index("chan"), 2)
    xs = lax.dynamic_slice_in_dim(x3, (1 - half) * (outer // 2), outer // 2, 0)
    xr = send(xs, 0, 1)
    blocks_other = send(blocks, 0, 1)
    twisted = seq_swap(right_pass(x3, right_factor, twiddle, seq))
    middle = middle_pass(s, x3, xr, blocks, blocks_other)
    middle = around(middle)
    pieces = mix_pass(s, mixer, middle)
    twisted, _ = lax.optimization_barrier((twisted, pieces[0]))
    mixed_wire = left_pass(left_factor, twisted)

    mixed = seq_swap(mixed_wire)
    pieces = across(pieces)
    gate3, grad_mixed = gate_pass(s, og3, pieces, seq)

    grad_mixed, mixed = lax.optimization_barrier((grad_mixed, mixed))
    grad_wire = seq_swap(grad_mixed)
    output, pieces = out_pass(s, mixed, gate3, og3)
    pieces = across(pieces)
    grad_middle = mix_back(s, mixer, pieces)
    grad_wire, _ = lax.optimization_barrier((grad_wire, grad_middle[0]))
    grad_wire = left_pass(left_factor.T, grad_wire)

    grad_middle = around(grad_middle)
    grad_twisted = seq_swap(grad_wire)
    own, other = [], []
    for d in (0, 1, 3, 2):
        mine, away = chan_pass(s, blocks, blocks_other, grad_middle[d])
        own.append(mine)
        other.append(send(away, 0, 1))
    own, other = ([v[i] for i in (0, 1, 3, 2)] for v in (own, other))
    input_grad = tail_pass(s, grad_twisted, right_factor.T, twiddle, own, other)
    return (output.reshape(inputs.shape), input_grad.reshape(inputs.shape))


def solution(mesh):
    return jax.shard_map(
        body,
        mesh=mesh,
        in_specs=(
            P("seq", "chan"),
            P("seq", None),
            P(),
            P(),
            P("chan", None),
            P(),
            P("seq", "chan"),
        ),
        out_specs=(P("seq", "chan"), P("seq", "chan")),
        check_vma=False,
    )
```

```python
import functools

import jax
import jax.numpy as jnp
from jax import lax
from jax.experimental import pallas as pl
from jax.experimental.pallas import tpu as pltpu
from jax.sharding import PartitionSpec as P


F32 = jnp.float32
BF16 = jnp.bfloat16
NY = 4


def _params(mib=32):
    return pltpu.CompilerParams(vmem_limit_bytes=min(mib << 20, 67043328))


def _hbm(shape):
    return pltpu.HBM(shape, BF16)


def _cost(flops, nbytes):
    return pl.CostEstimate(flops=flops, bytes_accessed=nbytes, transcendentals=0)


def _fwd(s, d):
    return lax.rem(s[0] // 2 + d, NY)


def _back(s, d):
    return lax.rem(s[0] // 2 + NY - d, NY)


def _column(row, length):
    return jnp.transpose(jnp.broadcast_to(row, (128, length)))


def right_kernel(x_ref, r_ref, tw_ref, out_ref, scr):
    outer, _, chan = x_ref.shape
    rows = r_ref.shape[0]
    for a in range(outer):
        acc = jnp.dot(r_ref[...], x_ref[a], preferred_element_type=F32)
        col = _column(tw_ref[a : a + 1, :], rows)
        for c in range(chan // 128):
            scr[c, pl.ds(a, rows, stride=outer), :] = acc[:, c * 128 : c * 128 + 128] * col
    for c in range(chan // 128):
        out_ref[:, :, :, c * 128 : c * 128 + 128] = scr[c].reshape(*out_ref.shape[:3], 128).astype(BF16)


def right_pass(x3, right, twiddle, seq):
    outer, inner, chan = x3.shape
    steps = 2
    rows = inner // steps
    per = inner // seq
    return pl.pallas_call(
        right_kernel,
        name="right_pass",
        grid=(steps,),
        in_specs=[
            pl.BlockSpec((outer, inner, chan), lambda g: (0, 0, 0)),
            pl.BlockSpec((rows, inner), lambda g: (g, 0)),
            pl.BlockSpec((outer, rows), lambda g: (0, g)),
        ],
        out_specs=pl.BlockSpec((seq // steps, per, outer, chan), lambda g: (g, 0, 0, 0)),
        out_shape=_hbm((seq, per, outer, chan)),
        scratch_shapes=[pltpu.VMEM((chan // 128, rows * outer, 128), F32)],
        compiler_params=_params(64),
        cost_estimate=_cost(2 * outer * inner * inner * chan, 6 << 20),
    )(x3, right, twiddle)


def left_kernel(l_ref, in_ref, out_ref):
    seq, per, outer, chan = in_ref.shape
    for j in range(per):
        block = in_ref[:, j].astype(F32).reshape(seq * outer, chan).astype(BF16)
        acc = jnp.dot(l_ref[...], block, preferred_element_type=F32)
        out_ref[:, j] = acc.reshape(seq, outer, chan).astype(BF16)


def left_pass(left, wire):
    seq, per, outer, chan = wire.shape
    steps = 4
    full = seq * outer
    block = (seq, per // steps, outer, chan)
    return pl.pallas_call(
        left_kernel,
        name="left_pass",
        grid=(steps,),
        in_specs=[
            pl.BlockSpec((full, full), lambda g: (0, 0)),
            pl.BlockSpec(block, lambda g: (0, g, 0, 0)),
        ],
        out_specs=pl.BlockSpec(block, lambda g: (0, g, 0, 0)),
        out_shape=_hbm(wire.shape),
        compiler_params=_params(),
        cost_estimate=_cost(2 * full * full * per * chan, 4 << 20),
    )(left, wire)


def middle_kernel(s, x_ref, xp_ref, b_ref, *outs):
    d = pl.program_id(0)
    outer, rows, chan = x_ref.shape
    half = lax.rem(s[0], 2)
    own = b_ref[:, pl.ds(pl.multiple_of(half * chan, 128), chan)]
    other = b_ref[:, pl.ds(pl.multiple_of((1 - half) * chan, 128), chan)]
    dims = (((1,), (1,)), ((), ()))
    acc = lax.dot_general(x_ref[...].reshape(outer * rows, chan), own, dims, preferred_element_type=F32)
    acc += lax.dot_general(xp_ref[...].reshape(outer * rows, chan), other, dims, preferred_element_type=F32)
    value = acc.astype(BF16).reshape(outer, rows, chan)
    for i in range(NY):

        @pl.when(d == i)
        def _():
            outs[i][...] = value


def middle_pass(s, x3, xp3, blocks):
    outer, inner, chan = x3.shape
    rows = inner // NY
    block = (outer, rows, chan)
    return pl.pallas_call(
        middle_kernel,
        name="middle_pass",
        grid_spec=pltpu.PrefetchScalarGridSpec(
            num_scalar_prefetch=1,
            grid=(NY,),
            in_specs=[
                pl.BlockSpec(block, lambda d, s: (0, _fwd(s, d), 0)),
                pl.BlockSpec(block, lambda d, s: (0, _fwd(s, d), 0)),
                pl.BlockSpec(blocks.shape, lambda d, s: (0, 0)),
            ],
            out_specs=[pl.BlockSpec(block, lambda d, s: (0, 0, 0))] * NY,
        ),
        out_shape=[_hbm(block)] * NY,
        compiler_params=_params(),
        cost_estimate=_cost(4 * outer * inner * chan * chan, 6 << 20),
    )(s, x3, xp3, blocks)


def mix_kernel(flip, s, mix_ref, *refs):
    ins, outs = refs[:NY], refs[NY:]
    y = s[0] // 2
    values = [r[...].astype(F32) for r in ins]
    for e in range(NY):
        to = lax.rem(y + e, NY)
        acc = None
        for d in range(NY):
            frm = lax.rem(y + NY - d, NY)
            row = mix_ref[frm, pl.ds(to, 1), :] if flip else mix_ref[to, pl.ds(frm, 1), :]
            term = values[d] * row
            acc = term if acc is None else acc + term
        outs[e][...] = acc.astype(BF16)


def mix_pass(s, mixer, parts, flip):
    outer, rows, chan = parts[0].shape
    total = outer * rows
    steps = 4
    block = pl.BlockSpec((total // steps, chan), lambda g, s: (g, 0))
    outs = pl.pallas_call(
        functools.partial(mix_kernel, flip),
        name="mix_back" if flip else "mix_pass",
        grid_spec=pltpu.PrefetchScalarGridSpec(
            num_scalar_prefetch=1,
            grid=(steps,),
            in_specs=[pl.BlockSpec((NY, NY, chan), lambda g, s: (0, 0, lax.rem(s[0], 2)))] + [block] * NY,
            out_specs=[block] * NY,
        ),
        out_shape=[_hbm((total, chan))] * NY,
        compiler_params=_params(),
        cost_estimate=_cost(2 * NY * NY * total * chan, 4 << 20),
    )(s, mixer, *[p.reshape(total, chan) for p in parts])
    return [o.reshape(outer, rows, chan) for o in outs]


def gate_kernel(s, og_ref, g0, g1, g2, g3, gate_ref, wire_ref, scr):
    d = pl.program_id(0)
    outer, rows, chan = og_ref.shape
    for i, g_ref in enumerate((g0, g1, g2, g3)):

        @pl.when(d == i)
        def _():
            for a in range(outer):
                g = g_ref[a]
                gate_ref[a] = g
                for c in range(chan // 128):
                    cols = slice(c * 128, c * 128 + 128)
                    scr[c, pl.ds(a, rows, stride=outer), :] = og_ref[a, :, cols].astype(F32) * g[:, cols].astype(F32)

    for c in range(chan // 128):
        wire_ref[:, :, :, c * 128 : c * 128 + 128] = scr[c].reshape(*wire_ref.shape[:3], 128).astype(BF16)


def gate_pass(s, og3, parts, seq):
    outer, inner, chan = og3.shape
    rows = inner // NY
    per = inner // seq
    block = (outer, rows, chan)
    nat = pl.BlockSpec(block, lambda d, s: (0, _back(s, d), 0))
    return pl.pallas_call(
        gate_kernel,
        name="gate_pass",
        grid_spec=pltpu.PrefetchScalarGridSpec(
            num_scalar_prefetch=1,
            grid=(NY,),
            in_specs=[nat] + [pl.BlockSpec(block, lambda d, s: (0, 0, 0))] * NY,
            out_specs=[nat, pl.BlockSpec((seq // NY, per, outer, chan), lambda d, s: (_back(s, d), 0, 0, 0))],
            scratch_shapes=[pltpu.VMEM((chan // 128, rows * outer, 128), F32)],
        ),
        out_shape=[
            _hbm(og3.shape),
            _hbm((seq, per, outer, chan)),
        ],
        compiler_params=_params(),
        cost_estimate=_cost(outer * inner * chan, 8 << 20),
    )(s, og3, *parts)


def out_kernel(s, wire_ref, gate_ref, og_ref, out_ref, o0, o1, o2, o3, scr):
    d = pl.program_id(0)
    outer, rows, chan = og_ref.shape
    for c in range(chan // 128):
        scr[c] = wire_ref[:, :, :, c * 128 : c * 128 + 128].astype(F32).reshape(scr.shape[1:])
    for i, gg_ref in enumerate((o0, o1, o2, o3)):

        @pl.when(d == i)
        def _():
            for a in range(outer):
                for c in range(chan // 128):
                    cols = slice(c * 128, c * 128 + 128)
                    m = scr[c, pl.ds(a, rows, stride=outer), :]
                    out_ref[a, :, cols] = (gate_ref[a, :, cols].astype(F32) * m).astype(BF16)
                    gg_ref[a, :, cols] = (og_ref[a, :, cols].astype(F32) * m).astype(BF16)


def out_pass(s, wire, gate3, og3):
    outer, inner, chan = og3.shape
    seq, per = wire.shape[:2]
    rows = inner // NY
    block = (outer, rows, chan)
    nat = pl.BlockSpec(block, lambda d, s: (0, _fwd(s, d), 0))
    res = pl.pallas_call(
        out_kernel,
        name="out_pass",
        grid_spec=pltpu.PrefetchScalarGridSpec(
            num_scalar_prefetch=1,
            grid=(NY,),
            in_specs=[pl.BlockSpec((seq // NY, per, outer, chan), lambda d, s: (_fwd(s, d), 0, 0, 0)), nat, nat],
            out_specs=[nat] + [pl.BlockSpec(block, lambda d, s: (0, 0, 0))] * NY,
            scratch_shapes=[pltpu.VMEM((chan // 128, rows * outer, 128), F32)],
        ),
        out_shape=[_hbm(og3.shape)] + [_hbm(block)] * NY,
        compiler_params=_params(),
        cost_estimate=_cost(2 * outer * inner * chan, 10 << 20),
    )(s, wire, gate3, og3)
    return res[0], res[1:]


def chan_kernel(s, b_ref, bo_ref, own_ref, other_ref, out_ref):
    chan = out_ref.shape[1]
    cols = pl.ds(pl.multiple_of(lax.rem(s[0], 2) * chan, 128), chan)
    acc = jnp.dot(own_ref[...], b_ref[:, cols], preferred_element_type=F32)
    acc += jnp.dot(other_ref[...], bo_ref[:, cols], preferred_element_type=F32)
    out_ref[...] = acc.astype(BF16)


def chan_pass(s, blocks, blocks_other, own, other):
    outer, rows, chan = own.shape
    total = outer * rows
    steps = 2
    whole = pl.BlockSpec(blocks.shape, lambda i, s: (0, 0))
    tile = pl.BlockSpec((total // steps, chan), lambda i, s: (i, 0))
    return pl.pallas_call(
        chan_kernel,
        name="chan_pass",
        grid_spec=pltpu.PrefetchScalarGridSpec(
            num_scalar_prefetch=1,
            grid=(steps,),
            in_specs=[whole, whole, tile, tile],
            out_specs=tile,
        ),
        out_shape=_hbm((total, chan)),
        compiler_params=_params(),
        cost_estimate=_cost(4 * total * chan * chan, 2 << 20),
    )(s, blocks, blocks_other, own.reshape(total, chan), other.reshape(total, chan))


def tail_kernel(s, wire_ref, rt_ref, tw_ref, *refs):
    parts, (out_ref, scr, total_ref) = refs[:NY], refs[NY:]
    outer, inner = tw_ref.shape
    chan = out_ref.shape[2]
    rows = inner // NY
    a = pl.program_id(0)

    @pl.when(a == 0)
    def _():
        for c in range(chan // 128):
            scr[c] = wire_ref[:, :, :, c * 128 : c * 128 + 128].astype(F32).reshape(scr.shape[1:])

    col = _column(tw_ref[pl.ds(a, 1), :], inner)
    grad = [(scr[c, pl.ds(a, inner, stride=outer), :] * col).astype(BF16) for c in range(chan // 128)]
    total_ref[...] = jnp.dot(rt_ref[...], jnp.concatenate(grad, axis=1), preferred_element_type=F32)
    for d in range(NY):
        at = pl.ds(pl.multiple_of(_back(s, d) * rows, rows), rows)
        out_ref[0, at, :] = (total_ref[at, :] + parts[d][...].astype(F32)).astype(BF16)


def tail_pass(s, wire, right_t, twiddle, parts):
    outer, inner = twiddle.shape
    chan = wire.shape[3]
    part = pl.BlockSpec((inner // NY, chan), lambda a, s: (a, 0))
    return pl.pallas_call(
        tail_kernel,
        name="tail_pass",
        grid_spec=pltpu.PrefetchScalarGridSpec(
            num_scalar_prefetch=1,
            grid=(outer,),
            in_specs=[
                pl.BlockSpec(wire.shape, lambda a, s: (0, 0, 0, 0)),
                pl.BlockSpec(right_t.shape, lambda a, s: (0, 0)),
                pl.BlockSpec(twiddle.shape, lambda a, s: (0, 0)),
            ]
            + [part] * NY,
            out_specs=pl.BlockSpec((1, inner, chan), lambda a, s: (a, 0, 0)),
            scratch_shapes=[pltpu.VMEM((chan // 128, outer * inner, 128), F32), pltpu.VMEM((inner, chan), F32)],
        ),
        out_shape=jax.ShapeDtypeStruct((outer, inner, chan), BF16),
        compiler_params=_params(64),
        cost_estimate=_cost(2 * outer * inner * inner * chan, 7 << 20),
    )(s, wire, right_t, twiddle, *parts)


def seq_swap(wire):
    return lax.all_to_all(wire, "seq", split_axis=0, concat_axis=0, tiled=True)


def body(inputs, twiddle, right_factor, left_factor, blocks, block_mixer, out_grad):
    outer, inner = twiddle.shape
    chan = inputs.shape[1]
    seq = left_factor.shape[0] // outer
    n = 2 * NY

    def to_pair(v):
        return lax.ppermute(v, "chan", [(c, c ^ 1) for c in range(n)])

    def around(parts):
        return [parts[0]] + [
            lax.ppermute(parts[d], "chan", [(c, (c + 2 * d) % n) for c in range(n)]) for d in range(1, NY)
        ]

    s = lax.axis_index("chan").reshape(1)
    x3 = inputs.reshape(outer, inner, chan)
    og3 = out_grad.reshape(outer, inner, chan)
    mixer = jnp.transpose(block_mixer, (1, 2, 0))

    xp3 = to_pair(inputs).reshape(x3.shape)
    twisted = seq_swap(right_pass(x3, right_factor, twiddle, seq))
    middle = middle_pass(s, x3, xp3, blocks)
    middle = around(middle)
    mixed_wire = left_pass(left_factor, twisted)

    mixed = seq_swap(mixed_wire)
    pieces = around(mix_pass(s, mixer, middle, False))
    gate3, grad_mixed = gate_pass(s, og3, pieces, seq)

    grad_mixed, mixed = lax.optimization_barrier((grad_mixed, mixed))
    grad_wire = seq_swap(grad_mixed)
    output, pieces = out_pass(s, mixed, gate3, og3)
    grad_middle = mix_pass(s, mixer, around(pieces), True)
    grad_wire = left_pass(left_factor.T, grad_wire)
    blocks_other = to_pair(blocks)

    grad_middle = around(grad_middle)
    grad_twisted = seq_swap(grad_wire)
    parts = [None] * NY
    for d in (0, 1, 3, 2):
        parts[d] = chan_pass(s, blocks, blocks_other, grad_middle[d], to_pair(grad_middle[d]))
    input_grad = tail_pass(s, grad_twisted, right_factor.T, twiddle, parts)
    return (output.reshape(inputs.shape), input_grad.reshape(inputs.shape))


def solution(mesh):
    return jax.shard_map(
        body,
        mesh=mesh,
        in_specs=(
            P("seq", "chan"),
            P("seq", None),
            P(),
            P(),
            P("chan", None),
            P(),
            P("seq", "chan"),
        ),
        out_specs=(P("seq", "chan"), P("seq", "chan")),
        check_vma=False,
    )
```

```python
import functools

import jax
import jax.numpy as jnp
from jax import lax
from jax.experimental import pallas as pl
from jax.experimental.pallas import tpu as pltpu
from jax.sharding import PartitionSpec as P


F32 = jnp.float32
BF16 = jnp.bfloat16
NY = 4
CHUNKS = 2


def _params(mib=32):
    return pltpu.CompilerParams(vmem_limit_bytes=min(mib << 20, 67043328))


def _hbm(shape):
    return pltpu.HBM(shape, BF16)


def _cost(flops, nbytes):
    return pl.CostEstimate(flops=flops, bytes_accessed=nbytes, transcendentals=0)


def _fwd(s, d):
    return lax.rem(s[0] // 2 + d, NY)


def _back(s, d):
    return lax.rem(s[0] // 2 + NY - d, NY)


def _column(row, length):
    return jnp.transpose(jnp.broadcast_to(row, (128, length)))


def right_kernel(x_ref, r_ref, tw_ref, out_ref, scr):
    outer, _, chan = x_ref.shape
    rows = r_ref.shape[0]
    for a in range(outer):
        acc = jnp.dot(r_ref[...], x_ref[a], preferred_element_type=F32)
        col = _column(tw_ref[a : a + 1, :], rows)
        for c in range(chan // 128):
            scr[c, pl.ds(a, rows, stride=outer), :] = acc[:, c * 128 : c * 128 + 128] * col
    for c in range(chan // 128):
        out_ref[:, :, :, c * 128 : c * 128 + 128] = scr[c].reshape(*out_ref.shape[:3], 128).astype(BF16)


def right_pass(x3, right, twiddle, seq):
    outer, inner, chan = x3.shape
    steps = 2
    rows = inner // steps
    per = inner // seq
    return pl.pallas_call(
        right_kernel,
        name="right_pass",
        grid=(steps,),
        in_specs=[
            pl.BlockSpec((outer, inner, chan), lambda g: (0, 0, 0)),
            pl.BlockSpec((rows, inner), lambda g: (g, 0)),
            pl.BlockSpec((outer, rows), lambda g: (0, g)),
        ],
        out_specs=pl.BlockSpec((seq // steps, per, outer, chan), lambda g: (g, 0, 0, 0)),
        out_shape=_hbm((seq, per, outer, chan)),
        scratch_shapes=[pltpu.VMEM((chan // 128, rows * outer, 128), F32)],
        compiler_params=_params(64),
        cost_estimate=_cost(2 * outer * inner * inner * chan, 6 << 20),
    )(x3, right, twiddle)


def left_kernel(l_ref, in_ref, out_ref):
    seq, per, outer, chan = in_ref.shape
    for j in range(per):
        block = in_ref[:, j].astype(F32).reshape(seq * outer, chan).astype(BF16)
        acc = jnp.dot(l_ref[...], block, preferred_element_type=F32)
        out_ref[:, j] = acc.reshape(seq, outer, chan).astype(BF16)


def left_pass(left, wire):
    seq, per, outer, chan = wire.shape
    steps = 8
    full = seq * outer
    block = (seq, per // steps, outer, chan)
    return pl.pallas_call(
        left_kernel,
        name="left_pass",
        grid=(steps,),
        in_specs=[
            pl.BlockSpec((full, full), lambda g: (0, 0)),
            pl.BlockSpec(block, lambda g: (0, g, 0, 0)),
        ],
        out_specs=pl.BlockSpec(block, lambda g: (0, g, 0, 0)),
        out_shape=_hbm(wire.shape),
        compiler_params=_params(),
        cost_estimate=_cost(2 * full * full * per * chan, 4 << 20),
    )(left, wire)


def middle_kernel(s, x_ref, xp_ref, b_ref, *outs):
    d = pl.program_id(0)
    outer, rows, chan = x_ref.shape
    half = lax.rem(s[0], 2)
    own = b_ref[:, pl.ds(pl.multiple_of(half * chan, 128), chan)]
    other = b_ref[:, pl.ds(pl.multiple_of((1 - half) * chan, 128), chan)]
    dims = (((1,), (1,)), ((), ()))
    acc = lax.dot_general(x_ref[...].reshape(outer * rows, chan), own, dims, preferred_element_type=F32)
    acc += lax.dot_general(xp_ref[...].reshape(outer * rows, chan), other, dims, preferred_element_type=F32)
    value = acc.astype(BF16)
    for i in range(NY):

        @pl.when(d == i)
        def _():
            outs[i][...] = value


def middle_pass(s, x3, xp3, blocks, u):
    part, inner, chan = xp3.shape
    rows = inner // NY
    block = (part, rows, chan)
    out = (part * rows, chan)
    return pl.pallas_call(
        middle_kernel,
        name="middle_pass",
        grid_spec=pltpu.PrefetchScalarGridSpec(
            num_scalar_prefetch=1,
            grid=(NY,),
            in_specs=[
                pl.BlockSpec(block, lambda d, s: (u, _fwd(s, d), 0)),
                pl.BlockSpec(block, lambda d, s: (0, _fwd(s, d), 0)),
                pl.BlockSpec(blocks.shape, lambda d, s: (0, 0)),
            ],
            out_specs=[pl.BlockSpec(out, lambda d, s: (0, 0))] * NY,
        ),
        out_shape=[_hbm(out)] * NY,
        compiler_params=_params(),
        cost_estimate=_cost(4 * part * inner * chan * chan, 3 << 20),
    )(s, x3, xp3, blocks)


def mix_kernel(flip, s, mix_ref, *refs):
    ins, outs = refs[:NY], refs[NY:]
    y = s[0] // 2
    values = [r[...].astype(F32) for r in ins]
    for e in range(NY):
        to = lax.rem(y + e, NY)
        acc = None
        for d in range(NY):
            frm = lax.rem(y + NY - d, NY)
            row = mix_ref[frm, pl.ds(to, 1), :] if flip else mix_ref[to, pl.ds(frm, 1), :]
            term = values[d] * row
            acc = term if acc is None else acc + term
        outs[e][...] = acc.astype(BF16)


def mix_pass(s, mixer, parts, flip):
    total, chan = parts[0].shape
    steps = 2
    block = pl.BlockSpec((total // steps, chan), lambda g, s: (g, 0))
    return pl.pallas_call(
        functools.partial(mix_kernel, flip),
        name="mix_back" if flip else "mix_pass",
        grid_spec=pltpu.PrefetchScalarGridSpec(
            num_scalar_prefetch=1,
            grid=(steps,),
            in_specs=[pl.BlockSpec((NY, NY, chan), lambda g, s: (0, 0, lax.rem(s[0], 2)))] + [block] * NY,
            out_specs=[block] * NY,
        ),
        out_shape=[_hbm((total, chan))] * NY,
        compiler_params=_params(),
        cost_estimate=_cost(2 * NY * NY * total * chan, 2 << 20),
    )(s, mixer, *parts)


def gate_kernel(s, og_ref, *refs):
    pieces, (gate_ref, wire_ref, scr) = refs[: CHUNKS * NY], refs[CHUNKS * NY :]
    d = pl.program_id(0)
    outer, rows, chan = og_ref.shape
    part = outer // CHUNKS
    for i in range(NY):

        @pl.when(d == i)
        def _():
            for a in range(outer):
                at = (a % part) * rows
                g = pieces[a // part * NY + i][at : at + rows, :]
                gate_ref[a] = g
                for c in range(chan // 128):
                    cols = slice(c * 128, c * 128 + 128)
                    scr[c, pl.ds(a, rows, stride=outer), :] = og_ref[a, :, cols].astype(F32) * g[:, cols].astype(F32)

    for c in range(chan // 128):
        wire_ref[:, :, :, c * 128 : c * 128 + 128] = scr[c].reshape(*wire_ref.shape[:3], 128).astype(BF16)


def gate_pass(s, og3, pieces, seq):
    outer, inner, chan = og3.shape
    rows = inner // NY
    per = inner // seq
    block = (outer, rows, chan)
    nat = pl.BlockSpec(block, lambda d, s: (0, _back(s, d), 0))
    return pl.pallas_call(
        gate_kernel,
        name="gate_pass",
        grid_spec=pltpu.PrefetchScalarGridSpec(
            num_scalar_prefetch=1,
            grid=(NY,),
            in_specs=[nat] + [pl.BlockSpec(pieces[0].shape, lambda d, s: (0, 0))] * (CHUNKS * NY),
            out_specs=[nat, pl.BlockSpec((seq // NY, per, outer, chan), lambda d, s: (_back(s, d), 0, 0, 0))],
            scratch_shapes=[pltpu.VMEM((chan // 128, rows * outer, 128), F32)],
        ),
        out_shape=[
            _hbm(og3.shape),
            _hbm((seq, per, outer, chan)),
        ],
        compiler_params=_params(),
        cost_estimate=_cost(outer * inner * chan, 8 << 20),
    )(s, og3, *pieces)


def cot_kernel(s, wire_ref, og_ref, *refs):
    pieces, scr = refs[:NY], refs[NY]
    d = pl.program_id(0)
    outer, rows, chan = og_ref.shape
    for c in range(chan // 128):
        scr[c] = wire_ref[:, :, :, c * 128 : c * 128 + 128].astype(F32).reshape(scr.shape[1:])
    for i in range(NY):

        @pl.when(d == i)
        def _():
            for a in range(outer):
                for c in range(chan // 128):
                    cols = slice(c * 128, c * 128 + 128)
                    m = scr[c, pl.ds(a, rows, stride=outer), :]
                    pieces[i][a * rows : a * rows + rows, cols] = (og_ref[a, :, cols].astype(F32) * m).astype(BF16)


def cot_pass(s, wire, og3, u):
    outer, inner, chan = og3.shape
    seq, per = wire.shape[:2]
    parts = NY * CHUNKS
    rows = inner // parts
    piece = (outer * rows, chan)
    return pl.pallas_call(
        cot_kernel,
        name="cot_pass",
        grid_spec=pltpu.PrefetchScalarGridSpec(
            num_scalar_prefetch=1,
            grid=(NY,),
            in_specs=[
                pl.BlockSpec((seq // parts, per, outer, chan), lambda d, s: (_fwd(s, d) * CHUNKS + u, 0, 0, 0)),
                pl.BlockSpec((outer, rows, chan), lambda d, s: (0, _fwd(s, d) * CHUNKS + u, 0)),
            ],
            out_specs=[pl.BlockSpec(piece, lambda d, s: (0, 0))] * NY,
            scratch_shapes=[pltpu.VMEM((chan // 128, rows * outer, 128), F32)],
        ),
        out_shape=[_hbm(piece)] * NY,
        compiler_params=_params(),
        cost_estimate=_cost(outer * inner * chan // CHUNKS, 3 << 20),
    )(s, wire, og3)


def out_kernel(wire_ref, gate_ref, out_ref, scr):
    outer, rows, chan = out_ref.shape
    for c in range(chan // 128):
        scr[c] = wire_ref[:, :, :, c * 128 : c * 128 + 128].astype(F32).reshape(scr.shape[1:])
    for a in range(outer):
        for c in range(chan // 128):
            cols = slice(c * 128, c * 128 + 128)
            m = scr[c, pl.ds(a, rows, stride=outer), :]
            out_ref[a, :, cols] = (gate_ref[a, :, cols].astype(F32) * m).astype(BF16)


def out_pass(wire, gate3):
    outer, inner, chan = gate3.shape
    seq, per = wire.shape[:2]
    rows = inner // NY
    nat = pl.BlockSpec((outer, rows, chan), lambda d: (0, d, 0))
    return pl.pallas_call(
        out_kernel,
        name="out_pass",
        grid=(NY,),
        in_specs=[pl.BlockSpec((seq // NY, per, outer, chan), lambda d: (d, 0, 0, 0)), nat],
        out_specs=nat,
        out_shape=_hbm(gate3.shape),
        scratch_shapes=[pltpu.VMEM((chan // 128, rows * outer, 128), F32)],
        compiler_params=_params(),
        cost_estimate=_cost(outer * inner * chan, 6 << 20),
    )(wire, gate3)


def chan_kernel(s, b_ref, bo_ref, *refs):
    own, other, out_ref = refs[:NY], refs[NY : 2 * NY], refs[2 * NY]
    d = pl.program_id(0)
    chan = out_ref.shape[2]
    cols = pl.ds(pl.multiple_of(lax.rem(s[0], 2) * chan, 128), chan)
    for i in range(NY):

        @pl.when(d == i)
        def _():
            acc = jnp.dot(own[i][...], b_ref[:, cols], preferred_element_type=F32)
            acc += jnp.dot(other[i][...], bo_ref[:, cols], preferred_element_type=F32)
            out_ref[0] = acc.astype(BF16)


def chan_pass(s, blocks, blocks_other, own, other):
    total, chan = own[0].shape
    whole = pl.BlockSpec(blocks.shape, lambda d, s: (0, 0))
    tile = pl.BlockSpec((total, chan), lambda d, s: (0, 0))
    return pl.pallas_call(
        chan_kernel,
        name="chan_pass",
        grid_spec=pltpu.PrefetchScalarGridSpec(
            num_scalar_prefetch=1,
            grid=(NY,),
            in_specs=[whole, whole] + [tile] * (2 * NY),
            out_specs=pl.BlockSpec((1, total, chan), lambda d, s: (_back(s, d), 0, 0)),
        ),
        out_shape=_hbm((NY, total, chan)),
        compiler_params=_params(),
        cost_estimate=_cost(4 * NY * total * chan * chan, 3 << 20),
    )(s, blocks, blocks_other, *own, *other)


def tail_kernel(wire_ref, rt_ref, tw_ref, *refs):
    parts, (out_ref, scr) = refs[:CHUNKS], refs[CHUNKS:]
    outer, inner = tw_ref.shape
    chan = out_ref.shape[2]
    rows = inner // NY // CHUNKS
    a = pl.program_id(0)

    @pl.when(a == 0)
    def _():
        for c in range(chan // 128):
            scr[c] = wire_ref[:, :, :, c * 128 : c * 128 + 128].astype(F32).reshape(scr.shape[1:])

    col = _column(tw_ref[pl.ds(a, 1), :], inner)
    grad = [(scr[c, pl.ds(a, inner, stride=outer), :] * col).astype(BF16) for c in range(chan // 128)]
    acc = jnp.dot(rt_ref[...], jnp.concatenate(grad, axis=1), preferred_element_type=F32)
    for q in range(NY):
        for u in range(CHUNKS):
            at = (q * CHUNKS + u) * rows
            out_ref[0, at : at + rows, :] = (acc[at : at + rows] + parts[u][q].astype(F32)).astype(BF16)


def tail_pass(wire, right_t, twiddle, parts):
    outer, inner = twiddle.shape
    chan = wire.shape[3]
    part = pl.BlockSpec((NY, inner // NY // CHUNKS, chan), lambda a: (0, a, 0))
    return pl.pallas_call(
        tail_kernel,
        name="tail_pass",
        grid=(outer,),
        in_specs=[
            pl.BlockSpec(wire.shape, lambda a: (0, 0, 0, 0)),
            pl.BlockSpec(right_t.shape, lambda a: (0, 0)),
            pl.BlockSpec(twiddle.shape, lambda a: (0, 0)),
        ]
        + [part] * CHUNKS,
        out_specs=pl.BlockSpec((1, inner, chan), lambda a: (a, 0, 0)),
        scratch_shapes=[pltpu.VMEM((chan // 128, outer * inner, 128), F32)],
        out_shape=jax.ShapeDtypeStruct((outer, inner, chan), BF16),
        compiler_params=_params(64),
        cost_estimate=_cost(2 * outer * inner * inner * chan, 7 << 20),
    )(wire, right_t, twiddle, *parts)


def seq_swap(wire):
    return lax.all_to_all(wire, "seq", split_axis=0, concat_axis=0, tiled=True)


def body(inputs, twiddle, right_factor, left_factor, blocks, block_mixer, out_grad):
    outer, inner = twiddle.shape
    chan = inputs.shape[1]
    seq = left_factor.shape[0] // outer
    n = 2 * NY

    def to_pair(v):
        return lax.ppermute(v, "chan", [(c, c ^ 1) for c in range(n)])

    def around(parts):
        return [parts[0]] + [
            lax.ppermute(parts[d], "chan", [(c, (c + 2 * d) % n) for c in range(n)]) for d in range(1, NY)
        ]

    s = lax.axis_index("chan").reshape(1)
    x3 = inputs.reshape(outer, inner, chan)
    og3 = out_grad.reshape(outer, inner, chan)
    mixer = jnp.transpose(block_mixer, (1, 2, 0))

    part = outer // CHUNKS
    middle = []
    xp = to_pair(x3[:part])
    twisted = seq_swap(right_pass(x3, right_factor, twiddle, seq))
    middle.append(middle_pass(s, x3, xp, blocks, 0))
    later, _ = lax.optimization_barrier((x3, middle[0][0]))
    xp = to_pair(later[part:])
    middle.append(middle_pass(s, x3, xp, blocks, 1))
    mixed_wire = left_pass(left_factor, twisted)
    mixed = seq_swap(mixed_wire)
    pieces = []
    for u in range(CHUNKS):
        mixes = mix_pass(s, mixer, around(middle[u]), False)
        pieces += around(mixes)
    blocks_other = to_pair(blocks)
    gate3, grad_mixed = gate_pass(s, og3, pieces, seq)

    grad_mixed, mixed = lax.optimization_barrier((grad_mixed, mixed))
    grad_wire = seq_swap(grad_mixed)
    grads, others = [], []
    for u in range(CHUNKS):
        cots = cot_pass(s, mixed, og3, u)
        cots = around(cots)
        cots = mix_pass(s, mixer, cots, True)
        grads.append(around(cots))
        others.append([None] * NY)
        for d in (0, 1, 3, 2):
            others[u][d] = to_pair(grads[u][d])
    output = out_pass(mixed, gate3)
    grad_wire = left_pass(left_factor.T, grad_wire)
    grad_twisted = seq_swap(grad_wire)
    parts = []
    for u in range(CHUNKS):
        parts.append(chan_pass(s, blocks, blocks_other, grads[u], others[u]))
    input_grad = tail_pass(grad_twisted, right_factor.T, twiddle, parts)
    return (output.reshape(inputs.shape), input_grad.reshape(inputs.shape))


def solution(mesh):
    return jax.shard_map(
        body,
        mesh=mesh,
        in_specs=(
            P("seq", "chan"),
            P("seq", None),
            P(),
            P(),
            P("chan", None),
            P(),
            P("seq", "chan"),
        ),
        out_specs=(P("seq", "chan"), P("seq", "chan")),
        check_vma=False,
    )
```

```python
import functools

import jax
import jax.numpy as jnp
from jax import lax
from jax.experimental import pallas as pl
from jax.experimental.pallas import tpu as pltpu
from jax.sharding import PartitionSpec as P


F32 = jnp.float32
BF16 = jnp.bfloat16
NY = 4
CHUNKS = 2


def _params(mib=64):
    return pltpu.CompilerParams(vmem_limit_bytes=min(mib << 20, 67043328))


def _hbm(shape):
    return pltpu.HBM(shape, BF16)


def _cost(flops, nbytes):
    return pl.CostEstimate(flops=flops, bytes_accessed=nbytes, transcendentals=0)


def _fwd(s, d):
    return lax.rem(s[0] // 2 + d, NY)


def _back(s, d):
    return lax.rem(s[0] // 2 + NY - d, NY)


def _column(row, length):
    return jnp.transpose(jnp.broadcast_to(row, (128, length)))


def right_kernel(x_ref, r_ref, tw_ref, out_ref, first_ref, scr):
    outer, _, chan = x_ref.shape
    rows = r_ref.shape[0]
    at = pl.ds(pl.multiple_of(pl.program_id(0) * rows, rows), rows)
    first_ref[...] = x_ref[: first_ref.shape[0], at, :]
    for a in range(outer):
        acc = jnp.dot(r_ref[...], x_ref[a], preferred_element_type=F32)
        col = _column(tw_ref[a : a + 1, :], rows)
        for c in range(chan // 128):
            scr[c, pl.ds(a, rows, stride=outer), :] = acc[:, c * 128 : c * 128 + 128] * col
    for c in range(chan // 128):
        out_ref[:, :, :, c * 128 : c * 128 + 128] = scr[c].reshape(*out_ref.shape[:3], 128).astype(BF16)


def right_pass(x3, right, twiddle, seq):
    outer, inner, chan = x3.shape
    steps = 2
    rows = inner // steps
    per = inner // seq
    return pl.pallas_call(
        right_kernel,
        name="right_pass",
        grid=(steps,),
        in_specs=[
            pl.BlockSpec((outer, inner, chan), lambda g: (0, 0, 0)),
            pl.BlockSpec((rows, inner), lambda g: (g, 0)),
            pl.BlockSpec((outer, rows), lambda g: (0, g)),
        ],
        out_specs=[
            pl.BlockSpec((seq // steps, per, outer, chan), lambda g: (g, 0, 0, 0)),
            pl.BlockSpec((outer // CHUNKS, rows, chan), lambda g: (0, g, 0)),
        ],
        out_shape=[_hbm((seq, per, outer, chan)), _hbm((outer // CHUNKS, inner, chan))],
        scratch_shapes=[pltpu.VMEM((chan // 128, rows * outer, 128), F32)],
        compiler_params=_params(),
        cost_estimate=_cost(2 * outer * inner * inner * chan, 6 << 20),
    )(x3, right, twiddle)


def left_kernel(l_ref, in_ref, out_ref):
    seq, per, outer, chan = in_ref.shape
    for j in range(per):
        block = in_ref[:, j].astype(F32).reshape(seq * outer, chan).astype(BF16)
        acc = jnp.dot(l_ref[...], block, preferred_element_type=F32)
        out_ref[:, j] = acc.reshape(seq, outer, chan).astype(BF16)


def left_pass(left, wire):
    seq, per, outer, chan = wire.shape
    steps = 2
    full = seq * outer
    block = (seq, per // steps, outer, chan)
    return pl.pallas_call(
        left_kernel,
        name="left_pass",
        grid=(steps,),
        in_specs=[
            pl.BlockSpec((full, full), lambda g: (0, 0)),
            pl.BlockSpec(block, lambda g: (0, g, 0, 0)),
        ],
        out_specs=pl.BlockSpec(block, lambda g: (0, g, 0, 0)),
        out_shape=_hbm(wire.shape),
        compiler_params=_params(),
        cost_estimate=_cost(2 * full * full * per * chan, 4 << 20),
    )(left, wire)


def turn_kernel(in_ref, out_ref):
    out_ref[...] = jnp.transpose(in_ref[...].astype(F32)).astype(BF16)


def turn_pass(matrix):
    return pl.pallas_call(
        turn_kernel,
        name="turn_pass",
        out_shape=_hbm(matrix.shape),
        compiler_params=_params(),
        cost_estimate=_cost(0, 1 << 18),
    )(matrix)


def middle_kernel(s, x_ref, xp_ref, b_ref, *outs):
    d = pl.program_id(0)
    outer, rows, chan = x_ref.shape
    half = lax.rem(s[0], 2)
    own = b_ref[:, pl.ds(pl.multiple_of(half * chan, 128), chan)]
    other = b_ref[:, pl.ds(pl.multiple_of((1 - half) * chan, 128), chan)]
    dims = (((1,), (1,)), ((), ()))
    acc = lax.dot_general(x_ref[...].reshape(outer * rows, chan), own, dims, preferred_element_type=F32)
    acc += lax.dot_general(xp_ref[...].reshape(outer * rows, chan), other, dims, preferred_element_type=F32)
    value = acc.astype(BF16)
    for i in range(NY):

        @pl.when(d == i)
        def _():
            outs[i][...] = value


def middle_pass(s, x3, xp3, blocks, u):
    part, inner, chan = xp3.shape
    rows = inner // NY
    block = (part, rows, chan)
    out = (part * rows, chan)
    return pl.pallas_call(
        middle_kernel,
        name="middle_pass",
        grid_spec=pltpu.PrefetchScalarGridSpec(
            num_scalar_prefetch=1,
            grid=(NY,),
            in_specs=[
                pl.BlockSpec(block, lambda d, s: (u, _fwd(s, d), 0)),
                pl.BlockSpec(block, lambda d, s: (0, _fwd(s, d), 0)),
                pl.BlockSpec(blocks.shape, lambda d, s: (0, 0)),
            ],
            out_specs=[pl.BlockSpec(out, lambda d, s: (0, 0))] * NY,
        ),
        out_shape=[_hbm(out)] * NY,
        compiler_params=_params(),
        cost_estimate=_cost(4 * part * inner * chan * chan, 3 << 20),
    )(s, x3, xp3, blocks)


def mix_kernel(flip, s, mix_ref, *refs):
    ins, outs = refs[:NY], refs[NY:]
    y = s[0] // 2
    values = [r[...].astype(F32) for r in ins]
    for e in range(NY):
        to = lax.rem(y + e, NY)
        acc = None
        for d in range(NY):
            frm = lax.rem(y + NY - d, NY)
            row = mix_ref[frm, pl.ds(to, 1), :] if flip else mix_ref[to, pl.ds(frm, 1), :]
            term = values[d] * row
            acc = term if acc is None else acc + term
        outs[e][...] = acc.astype(BF16)


def mix_pass(s, mixer, parts, flip):
    total, chan = parts[0].shape
    steps = 2
    block = pl.BlockSpec((total // steps, chan), lambda g, s: (g, 0))
    return pl.pallas_call(
        functools.partial(mix_kernel, flip),
        name="mix_back" if flip else "mix_pass",
        grid_spec=pltpu.PrefetchScalarGridSpec(
            num_scalar_prefetch=1,
            grid=(steps,),
            in_specs=[pl.BlockSpec((NY, NY, chan), lambda g, s: (0, 0, lax.rem(s[0], 2)))] + [block] * NY,
            out_specs=[block] * NY,
        ),
        out_shape=[_hbm((total, chan))] * NY,
        compiler_params=_params(),
        cost_estimate=_cost(2 * NY * NY * total * chan, 2 << 20),
    )(s, mixer, *parts)


def gate_kernel(s, og_ref, *refs):
    pieces, (gate_ref, wire_ref, scr) = refs[: CHUNKS * NY], refs[CHUNKS * NY :]
    d = pl.program_id(0)
    outer, rows, chan = og_ref.shape
    part = outer // CHUNKS
    for i in range(NY):

        @pl.when(d == i)
        def _():
            for a in range(outer):
                at = (a % part) * rows
                g = pieces[a // part * NY + i][at : at + rows, :]
                gate_ref[a] = g
                for c in range(chan // 128):
                    cols = slice(c * 128, c * 128 + 128)
                    scr[c, pl.ds(a, rows, stride=outer), :] = og_ref[a, :, cols].astype(F32) * g[:, cols].astype(F32)

    for c in range(chan // 128):
        wire_ref[:, :, :, c * 128 : c * 128 + 128] = scr[c].reshape(*wire_ref.shape[:3], 128).astype(BF16)


def gate_pass(s, og3, pieces, seq):
    outer, inner, chan = og3.shape
    rows = inner // NY
    per = inner // seq
    block = (outer, rows, chan)
    nat = pl.BlockSpec(block, lambda d, s: (0, _back(s, d), 0))
    return pl.pallas_call(
        gate_kernel,
        name="gate_pass",
        grid_spec=pltpu.PrefetchScalarGridSpec(
            num_scalar_prefetch=1,
            grid=(NY,),
            in_specs=[nat] + [pl.BlockSpec(pieces[0].shape, lambda d, s: (0, 0))] * (CHUNKS * NY),
            out_specs=[nat, pl.BlockSpec((seq // NY, per, outer, chan), lambda d, s: (_back(s, d), 0, 0, 0))],
            scratch_shapes=[pltpu.VMEM((chan // 128, rows * outer, 128), F32)],
        ),
        out_shape=[
            _hbm(og3.shape),
            _hbm((seq, per, outer, chan)),
        ],
        compiler_params=_params(),
        cost_estimate=_cost(outer * inner * chan, 8 << 20),
    )(s, og3, *pieces)


def cot_kernel(s, wire_ref, og_ref, *refs):
    pieces, scr = refs[:NY], refs[NY]
    d = pl.program_id(0)
    outer, rows, chan = og_ref.shape
    for c in range(chan // 128):
        scr[c] = wire_ref[:, :, :, c * 128 : c * 128 + 128].astype(F32).reshape(scr.shape[1:])
    for i in range(NY):

        @pl.when(d == i)
        def _():
            for a in range(outer):
                for c in range(chan // 128):
                    cols = slice(c * 128, c * 128 + 128)
                    m = scr[c, pl.ds(a, rows, stride=outer), :]
                    pieces[i][a * rows : a * rows + rows, cols] = (og_ref[a, :, cols].astype(F32) * m).astype(BF16)


def cot_pass(s, wire, og3, u):
    outer, inner, chan = og3.shape
    seq, per = wire.shape[:2]
    parts = NY * CHUNKS
    rows = inner // parts
    piece = (outer * rows, chan)
    return pl.pallas_call(
        cot_kernel,
        name="cot_pass",
        grid_spec=pltpu.PrefetchScalarGridSpec(
            num_scalar_prefetch=1,
            grid=(NY,),
            in_specs=[
                pl.BlockSpec((seq // parts, per, outer, chan), lambda d, s: (_fwd(s, d) * CHUNKS + u, 0, 0, 0)),
                pl.BlockSpec((outer, rows, chan), lambda d, s: (0, _fwd(s, d) * CHUNKS + u, 0)),
            ],
            out_specs=[pl.BlockSpec(piece, lambda d, s: (0, 0))] * NY,
            scratch_shapes=[pltpu.VMEM((chan // 128, rows * outer, 128), F32)],
        ),
        out_shape=[_hbm(piece)] * NY,
        compiler_params=_params(),
        cost_estimate=_cost(outer * inner * chan // CHUNKS, 3 << 20),
    )(s, wire, og3)


def out_kernel(wire_ref, gate_ref, out_ref, scr):
    outer, rows, chan = out_ref.shape
    for c in range(chan // 128):
        scr[c] = wire_ref[:, :, :, c * 128 : c * 128 + 128].astype(F32).reshape(scr.shape[1:])
    for a in range(outer):
        for c in range(chan // 128):
            cols = slice(c * 128, c * 128 + 128)
            m = scr[c, pl.ds(a, rows, stride=outer), :]
            out_ref[a, :, cols] = (gate_ref[a, :, cols].astype(F32) * m).astype(BF16)


def out_pass(wire, gate3):
    outer, inner, chan = gate3.shape
    seq, per = wire.shape[:2]
    rows = inner // NY
    nat = pl.BlockSpec((outer, rows, chan), lambda d: (0, d, 0))
    return pl.pallas_call(
        out_kernel,
        name="out_pass",
        grid=(NY,),
        in_specs=[pl.BlockSpec((seq // NY, per, outer, chan), lambda d: (d, 0, 0, 0)), nat],
        out_specs=nat,
        out_shape=_hbm(gate3.shape),
        scratch_shapes=[pltpu.VMEM((chan // 128, rows * outer, 128), F32)],
        compiler_params=_params(),
        cost_estimate=_cost(outer * inner * chan, 6 << 20),
    )(wire, gate3)


def chan_kernel(s, b_ref, bo_ref, *refs):
    own, other, out_ref = refs[:NY], refs[NY : 2 * NY], refs[2 * NY]
    d = pl.program_id(0)
    chan = out_ref.shape[2]
    cols = pl.ds(pl.multiple_of(lax.rem(s[0], 2) * chan, 128), chan)
    for i in range(NY):

        @pl.when(d == i)
        def _():
            acc = jnp.dot(own[i][...], b_ref[:, cols], preferred_element_type=F32)
            acc += jnp.dot(other[i][...], bo_ref[:, cols], preferred_element_type=F32)
            out_ref[0] = acc.astype(BF16)


def chan_pass(s, blocks, blocks_other, own, other):
    total, chan = own[0].shape
    whole = pl.BlockSpec(blocks.shape, lambda d, s: (0, 0))
    tile = pl.BlockSpec((total, chan), lambda d, s: (0, 0))
    return pl.pallas_call(
        chan_kernel,
        name="chan_pass",
        grid_spec=pltpu.PrefetchScalarGridSpec(
            num_scalar_prefetch=1,
            grid=(NY,),
            in_specs=[whole, whole] + [tile] * (2 * NY),
            out_specs=pl.BlockSpec((1, total, chan), lambda d, s: (_back(s, d), 0, 0)),
        ),
        out_shape=_hbm((NY, total, chan)),
        compiler_params=_params(),
        cost_estimate=_cost(4 * NY * total * chan * chan, 3 << 20),
    )(s, blocks, blocks_other, *own, *other)


def tail_kernel(group, wire_ref, rt_ref, tw_ref, *refs):
    parts, (out_ref, scr) = refs[:CHUNKS], refs[CHUNKS:]
    outer, inner = tw_ref.shape
    chan = out_ref.shape[2]
    rows = inner // NY // CHUNKS
    g = pl.program_id(0)

    @pl.when(g == 0)
    def _():
        for c in range(chan // 128):
            scr[c] = wire_ref[:, :, :, c * 128 : c * 128 + 128].astype(F32).reshape(scr.shape[1:])

    for k in range(group):
        a = g * group + k
        col = _column(tw_ref[pl.ds(a, 1), :], inner)
        grad = [(scr[c, pl.ds(a, inner, stride=outer), :] * col).astype(BF16) for c in range(chan // 128)]
        acc = jnp.dot(rt_ref[...], jnp.concatenate(grad, axis=1), preferred_element_type=F32)
        for q in range(NY):
            for u in range(CHUNKS):
                at = (q * CHUNKS + u) * rows
                part = parts[u][q, k * rows : k * rows + rows].astype(F32)
                out_ref[k, at : at + rows, :] = (acc[at : at + rows] + part).astype(BF16)


def tail_pass(wire, right_t, twiddle, parts):
    outer, inner = twiddle.shape
    chan = wire.shape[3]
    group = outer // 2
    part = pl.BlockSpec((NY, group * inner // NY // CHUNKS, chan), lambda g: (0, g, 0))
    return pl.pallas_call(
        functools.partial(tail_kernel, group),
        name="tail_pass",
        grid=(outer // group,),
        in_specs=[
            pl.BlockSpec(wire.shape, lambda g: (0, 0, 0, 0)),
            pl.BlockSpec(right_t.shape, lambda g: (0, 0)),
            pl.BlockSpec(twiddle.shape, lambda g: (0, 0)),
        ]
        + [part] * CHUNKS,
        out_specs=pl.BlockSpec((group, inner, chan), lambda g: (g, 0, 0)),
        scratch_shapes=[pltpu.VMEM((chan // 128, outer * inner, 128), F32)],
        out_shape=jax.ShapeDtypeStruct((outer, inner, chan), BF16),
        compiler_params=_params(),
        cost_estimate=_cost(2 * outer * inner * inner * chan, 7 << 20),
    )(wire, right_t, twiddle, *parts)


def seq_swap(wire):
    return lax.all_to_all(wire, "seq", split_axis=0, concat_axis=0, tiled=True)


def body(inputs, twiddle, right_factor, left_factor, blocks, block_mixer, out_grad):
    outer, inner = twiddle.shape
    chan = inputs.shape[1]
    seq = left_factor.shape[0] // outer
    n = 2 * NY

    def to_pair(v):
        return lax.ppermute(v, "chan", [(c, c ^ 1) for c in range(n)])

    def around(parts):
        return [parts[0]] + [
            lax.ppermute(parts[d], "chan", [(c, (c + 2 * d) % n) for c in range(n)]) for d in range(1, NY)
        ]

    s = lax.axis_index("chan").reshape(1)
    x3 = inputs.reshape(outer, inner, chan)
    og3 = out_grad.reshape(outer, inner, chan)
    mixer = jnp.transpose(block_mixer, (1, 2, 0))

    part = outer // CHUNKS
    middle = []
    twisted, first = right_pass(x3, right_factor, twiddle, seq)
    xp = to_pair(first)
    left_t = turn_pass(left_factor)
    twisted = seq_swap(twisted)
    middle.append(middle_pass(s, x3, xp, blocks, 0))
    later, _ = lax.optimization_barrier((x3, middle[0][0]))
    xp = to_pair(later[part:])
    middle.append(middle_pass(s, x3, xp, blocks, 1))
    mixed_wire = left_pass(left_factor, twisted)
    mixed = seq_swap(mixed_wire)
    pieces = []
    for u in range(CHUNKS):
        mixes = mix_pass(s, mixer, around(middle[u]), False)
        pieces += around(mixes)
    blocks_other = to_pair(blocks)
    gate3, grad_mixed = gate_pass(s, og3, pieces, seq)

    grad_mixed, mixed = lax.optimization_barrier((grad_mixed, mixed))
    grad_wire = seq_swap(grad_mixed)
    grads, others = [], []
    for u in range(CHUNKS):
        cots = cot_pass(s, mixed, og3, u)
        cots = around(cots)
        cots = mix_pass(s, mixer, cots, True)
        grads.append(around(cots))
        others.append([None] * NY)
        for d in (0, 1, 3, 2):
            others[u][d] = to_pair(grads[u][d])
    output = out_pass(mixed, gate3)
    grad_wire = left_pass(left_t, grad_wire)
    grad_twisted = seq_swap(grad_wire)
    parts = []
    for u in range(CHUNKS):
        parts.append(chan_pass(s, blocks, blocks_other, grads[u], others[u]))
    input_grad = tail_pass(grad_twisted, right_factor.T, twiddle, parts)
    return (output.reshape(inputs.shape), input_grad.reshape(inputs.shape))


def solution(mesh):
    return jax.shard_map(
        body,
        mesh=mesh,
        in_specs=(
            P("seq", "chan"),
            P("seq", None),
            P(),
            P(),
            P("chan", None),
            P(),
            P("seq", "chan"),
        ),
        out_specs=(P("seq", "chan"), P("seq", "chan")),
        check_vma=False,
    )
```

```python
import functools

import jax
import jax.numpy as jnp
from jax import lax
from jax.experimental import pallas as pl
from jax.experimental.pallas import tpu as pltpu
from jax.sharding import PartitionSpec as P


F32 = jnp.float32
BF16 = jnp.bfloat16
NY = 4
CHUNKS = 2


def _params(mib=64):
    return pltpu.CompilerParams(vmem_limit_bytes=min(mib << 20, 67043328))


def _hbm(shape):
    return pltpu.HBM(shape, BF16)


def _cost(flops, nbytes):
    return pl.CostEstimate(flops=flops, bytes_accessed=nbytes, transcendentals=0)


def _fwd(s, d):
    return lax.rem(s[0] // 2 + d, NY)


def _back(s, d):
    return lax.rem(s[0] // 2 + NY - d, NY)


def _column(row, length):
    return jnp.transpose(jnp.broadcast_to(row, (128, length)))


def right_kernel(x_ref, r_ref, tw_ref, out_ref, first_ref, scr):
    outer, _, chan = x_ref.shape
    rows = r_ref.shape[0]
    part = x_ref.shape[1] // (NY * CHUNKS)
    for k in range(first_ref.shape[1] // part):
        at = pl.multiple_of(pl.program_id(0) * rows, rows) + k * part * CHUNKS
        first_ref[:, k * part : k * part + part, :] = x_ref[:, pl.ds(at, part), :]
    for a in range(outer):
        acc = jnp.dot(r_ref[...], x_ref[a], preferred_element_type=F32)
        col = _column(tw_ref[a : a + 1, :], rows)
        for c in range(chan // 128):
            scr[c, pl.ds(a, rows, stride=outer), :] = acc[:, c * 128 : c * 128 + 128] * col
    for c in range(chan // 128):
        out_ref[:, :, :, c * 128 : c * 128 + 128] = scr[c].reshape(*out_ref.shape[:3], 128).astype(BF16)


def right_pass(x3, right, twiddle, seq):
    outer, inner, chan = x3.shape
    steps = 2
    rows = inner // steps
    per = inner // seq
    return pl.pallas_call(
        right_kernel,
        name="right",
        grid=(steps,),
        in_specs=[
            pl.BlockSpec((outer, inner, chan), lambda g: (0, 0, 0)),
            pl.BlockSpec((rows, inner), lambda g: (g, 0)),
            pl.BlockSpec((outer, rows), lambda g: (0, g)),
        ],
        out_specs=[
            pl.BlockSpec((seq // steps, per, outer, chan), lambda g: (g, 0, 0, 0)),
            pl.BlockSpec((outer, rows // CHUNKS, chan), lambda g: (0, g, 0)),
        ],
        out_shape=[_hbm((seq, per, outer, chan)), _hbm((outer, inner // CHUNKS, chan))],
        scratch_shapes=[pltpu.VMEM((chan // 128, rows * outer, 128), F32)],
        compiler_params=_params(),
        cost_estimate=_cost(2 * outer * inner * inner * chan, 6 << 20),
    )(x3, right, twiddle)


def left_kernel(l_ref, in_ref, out_ref):
    seq, per, outer, chan = in_ref.shape
    for j in range(per):
        block = in_ref[:, j].astype(F32).reshape(seq * outer, chan).astype(BF16)
        acc = jnp.dot(l_ref[...], block, preferred_element_type=F32)
        out_ref[:, j] = acc.reshape(seq, outer, chan).astype(BF16)


def left_pass(left, wire):
    seq, per, outer, chan = wire.shape
    steps = 2
    full = seq * outer
    block = (seq, per // steps, outer, chan)
    return pl.pallas_call(
        left_kernel,
        name="left",
        grid=(steps,),
        in_specs=[
            pl.BlockSpec((full, full), lambda g: (0, 0)),
            pl.BlockSpec(block, lambda g: (0, g, 0, 0)),
        ],
        out_specs=pl.BlockSpec(block, lambda g: (0, g, 0, 0)),
        out_shape=_hbm(wire.shape),
        compiler_params=_params(),
        cost_estimate=_cost(2 * full * full * per * chan, 4 << 20),
    )(left, wire)


def turn_kernel(in_ref, out_ref):
    out_ref[...] = jnp.transpose(in_ref[...].astype(F32)).astype(BF16)


def turn_pass(matrix):
    return pl.pallas_call(
        turn_kernel,
        name="turn",
        out_shape=_hbm(matrix.shape),
        compiler_params=_params(),
        cost_estimate=_cost(0, 1 << 18),
    )(matrix)


def pick_kernel(x_ref, out_ref):
    out_ref[...] = x_ref[...]


def pick_pass(x3, u):
    outer, inner, chan = x3.shape
    rows = inner // (NY * CHUNKS)
    x5 = x3.reshape(outer, NY, CHUNKS * rows, chan)
    out = pl.pallas_call(
        pick_kernel,
        name="pick",
        grid=(1,),
        in_specs=[pl.BlockSpec((outer, NY, rows, chan), lambda g: (0, 0, u, 0))],
        out_specs=pl.BlockSpec((outer, NY, rows, chan), lambda g: (0, 0, 0, 0)),
        out_shape=_hbm((outer, NY, rows, chan)),
        compiler_params=_params(),
        cost_estimate=_cost(0, 2 << 20),
    )(x5)
    return out.reshape(outer, NY * rows, chan)


def middle_kernel(s, x_ref, xp_ref, b_ref, *outs):
    outer, _, rows, chan = x_ref.shape
    half = lax.rem(s[0], 2)
    own = b_ref[:, pl.ds(pl.multiple_of(half * chan, 128), chan)]
    other = b_ref[:, pl.ds(pl.multiple_of((1 - half) * chan, 128), chan)]
    dims = (((1,), (1,)), ((), ()))
    for d in range(NY):
        q = _fwd(s, d)
        x = x_ref[:, pl.ds(q, 1)].reshape(outer * rows, chan)
        xp = xp_ref[:, pl.ds(q, 1)].reshape(outer * rows, chan)
        acc = lax.dot_general(x, own, dims, preferred_element_type=F32)
        acc += lax.dot_general(xp, other, dims, preferred_element_type=F32)
        outs[d][...] = acc.astype(BF16)


def middle_pass(s, x3, xp3, blocks, u):
    outer, inner, chan = x3.shape
    rows = inner // (NY * CHUNKS)
    block = (outer, NY, rows, chan)
    out = (outer * rows, chan)
    return pl.pallas_call(
        middle_kernel,
        name="middle",
        grid_spec=pltpu.PrefetchScalarGridSpec(
            num_scalar_prefetch=1,
            grid=(1,),
            in_specs=[
                pl.BlockSpec(block, lambda g, s: (0, 0, u, 0)),
                pl.BlockSpec(block, lambda g, s: (0, 0, 0, 0)),
                pl.BlockSpec(blocks.shape, lambda g, s: (0, 0)),
            ],
            out_specs=[pl.BlockSpec(out, lambda g, s: (0, 0))] * NY,
        ),
        out_shape=[_hbm(out)] * NY,
        compiler_params=_params(),
        cost_estimate=_cost(4 * outer * rows * NY * chan * chan, 3 << 20),
    )(s, x3.reshape(outer, NY, CHUNKS * rows, chan), xp3.reshape(block), blocks)


def mix_kernel(flip, s, mix_ref, *refs):
    ins, outs = refs[:NY], refs[NY:]
    y = s[0] // 2
    rows = 64

    def rows_of(g, _):
        at = pl.ds(pl.multiple_of(g * rows, rows), rows)
        values = [r[at, :].astype(F32) for r in ins]
        for e in range(NY):
            to = lax.rem(y + e, NY)
            acc = None
            for d in range(NY):
                frm = lax.rem(y + NY - d, NY)
                row = mix_ref[frm, pl.ds(to, 1), :] if flip else mix_ref[to, pl.ds(frm, 1), :]
                term = values[d] * row
                acc = term if acc is None else acc + term
            outs[e][at, :] = acc.astype(BF16)
        return _

    lax.fori_loop(0, ins[0].shape[0] // rows, rows_of, 0)


def mix_pass(s, mixer, parts, flip):
    total, chan = parts[0].shape
    steps = 1
    block = pl.BlockSpec((total // steps, chan), lambda g, s: (g, 0))
    return pl.pallas_call(
        functools.partial(mix_kernel, flip),
        name="mix",
        grid_spec=pltpu.PrefetchScalarGridSpec(
            num_scalar_prefetch=1,
            grid=(steps,),
            in_specs=[pl.BlockSpec((NY, NY, chan), lambda g, s: (0, 0, lax.rem(s[0], 2)))] + [block] * NY,
            out_specs=[block] * NY,
        ),
        out_shape=[_hbm((total, chan))] * NY,
        compiler_params=_params(),
        cost_estimate=_cost(2 * NY * NY * total * chan, 2 << 20),
    )(s, mixer, *parts)


def gate_kernel(s, og_ref, *refs):
    pieces = refs[:NY]
    gate_ref, wire_ref, scr = refs[-3:]
    outer, _, rows, chan = og_ref.shape

    def one(a, _):
        for d in range(NY):
            q = _back(s, d)
            g = pieces[d][pl.ds(pl.multiple_of(a * rows, rows), rows), :]
            gate_ref[a, q] = g
            for c in range(chan // 128):
                cols = slice(c * 128, c * 128 + 128)
                og = og_ref[a, q, :, cols].astype(F32)
                scr[d * (chan // 128) + c, pl.ds(a, rows, stride=outer), :] = og * g[:, cols].astype(F32)
        return _

    lax.fori_loop(0, outer, one, 0)
    for d in range(NY):
        for c in range(chan // 128):
            value = scr[d * (chan // 128) + c].reshape(*wire_ref.shape[1:4], 128).astype(BF16)
            wire_ref[_back(s, d), :, :, :, c * 128 : c * 128 + 128] = value


def gate_pass(s, og3, pieces, seq, u, before):
    outer, inner, chan = og3.shape
    rows = inner // (NY * CHUNKS)
    per = inner // seq
    nat_shape = (outer, NY, CHUNKS * rows, chan)
    wire_shape = (NY, seq // NY, per, outer, chan)
    nat = pl.BlockSpec((outer, NY, rows, chan), lambda g, s: (0, 0, u, 0))
    whole = pl.BlockSpec(pieces[0].shape, lambda g, s: (0, 0))
    wire = pl.BlockSpec((NY, seq // NY // CHUNKS, per, outer, chan), lambda g, s: (0, u, 0, 0, 0))
    return pl.pallas_call(
        gate_kernel,
        name="gate",
        grid_spec=pltpu.PrefetchScalarGridSpec(
            num_scalar_prefetch=1,
            grid=(1,),
            in_specs=[nat] + [whole] * NY + [pl.BlockSpec(memory_space=pl.ANY)] * len(before),
            out_specs=[nat, wire],
            scratch_shapes=[pltpu.VMEM((NY * (chan // 128), rows * outer, 128), F32)],
        ),
        out_shape=[_hbm(nat_shape), _hbm(wire_shape)],
        input_output_aliases={2 + NY + i: i for i in range(len(before))},
        compiler_params=_params(),
        cost_estimate=_cost(outer * rows * NY * chan, 4 << 20),
    )(s, og3.reshape(nat_shape), *pieces, *before)


def cot_kernel(s, wire_ref, og_ref, *refs):
    pieces, scr = refs[:NY], refs[NY]
    outer, _, rows, chan = og_ref.shape
    for d in range(NY):
        for c in range(chan // 128):
            cols = slice(c * 128, c * 128 + 128)
            value = wire_ref[_fwd(s, d), :, :, :, cols].astype(F32)
            scr[d * (chan // 128) + c] = value.reshape(scr.shape[1:])

    def one(a, _):
        at = pl.ds(pl.multiple_of(a * rows, rows), rows)
        for d in range(NY):
            for c in range(chan // 128):
                cols = slice(c * 128, c * 128 + 128)
                m = scr[d * (chan // 128) + c, pl.ds(a, rows, stride=outer), :]
                pieces[d][at, cols] = (og_ref[a, _fwd(s, d), :, cols].astype(F32) * m).astype(BF16)
        return _

    lax.fori_loop(0, outer, one, 0)


def cot_pass(s, wire, og3, u):
    outer, inner, chan = og3.shape
    seq, per = wire.shape[:2]
    rows = inner // (NY * CHUNKS)
    piece = (outer * rows, chan)
    return pl.pallas_call(
        cot_kernel,
        name="cot",
        grid_spec=pltpu.PrefetchScalarGridSpec(
            num_scalar_prefetch=1,
            grid=(1,),
            in_specs=[
                pl.BlockSpec((NY, seq // NY // CHUNKS, per, outer, chan), lambda g, s: (0, u, 0, 0, 0)),
                pl.BlockSpec((outer, NY, rows, chan), lambda g, s: (0, 0, u, 0)),
            ],
            out_specs=[pl.BlockSpec(piece, lambda g, s: (0, 0))] * NY,
            scratch_shapes=[pltpu.VMEM((NY * (chan // 128), rows * outer, 128), F32)],
        ),
        out_shape=[_hbm(piece)] * NY,
        compiler_params=_params(),
        cost_estimate=_cost(outer * rows * NY * chan, 3 << 20),
    )(s, wire.reshape(NY, seq // NY, per, outer, chan), og3.reshape(outer, NY, CHUNKS * rows, chan))


def out_kernel(wire_ref, gate_ref, out_ref, scr):
    outer, rows, chan = out_ref.shape
    for c in range(chan // 128):
        scr[c] = wire_ref[:, :, :, c * 128 : c * 128 + 128].astype(F32).reshape(scr.shape[1:])
    for a in range(outer):
        for c in range(chan // 128):
            cols = slice(c * 128, c * 128 + 128)
            m = scr[c, pl.ds(a, rows, stride=outer), :]
            out_ref[a, :, cols] = (gate_ref[a, :, cols].astype(F32) * m).astype(BF16)


def out_pass(wire, gate3):
    outer, inner, chan = gate3.shape
    seq, per = wire.shape[:2]
    rows = inner // NY
    nat = pl.BlockSpec((outer, rows, chan), lambda d: (0, d, 0))
    return pl.pallas_call(
        out_kernel,
        name="out",
        grid=(NY,),
        in_specs=[pl.BlockSpec((seq // NY, per, outer, chan), lambda d: (d, 0, 0, 0)), nat],
        out_specs=nat,
        out_shape=_hbm(gate3.shape),
        scratch_shapes=[pltpu.VMEM((chan // 128, rows * outer, 128), F32)],
        compiler_params=_params(),
        cost_estimate=_cost(outer * inner * chan, 6 << 20),
    )(wire, gate3)


def chan_kernel(ds, s, b_ref, bo_ref, *refs):
    n = len(ds)
    own, other, out_ref = refs[:n], refs[n : 2 * n], refs[-1]
    chan = out_ref.shape[2]
    cols = pl.ds(pl.multiple_of(lax.rem(s[0], 2) * chan, 128), chan)
    for i in range(n):
        acc = jnp.dot(own[i][...], b_ref[:, cols], preferred_element_type=F32)
        acc += jnp.dot(other[i][...], bo_ref[:, cols], preferred_element_type=F32)
        out_ref[0 if n == 1 else _back(s, ds[i])] = acc.astype(BF16)


def chan_pass(s, blocks, blocks_other, own, other, ds, before):
    total, chan = own[0].shape
    whole = pl.BlockSpec(blocks.shape, lambda g, s: (0, 0))
    tile = pl.BlockSpec((total, chan), lambda g, s: (0, 0))
    if len(ds) == 1:
        out = pl.BlockSpec((1, total, chan), lambda g, s: (_back(s, ds[0]), 0, 0))
    else:
        out = pl.BlockSpec((NY, total, chan), lambda g, s: (0, 0, 0))
    n = 2 * len(ds)
    return pl.pallas_call(
        functools.partial(chan_kernel, ds),
        name="chan",
        grid_spec=pltpu.PrefetchScalarGridSpec(
            num_scalar_prefetch=1,
            grid=(1,),
            in_specs=[whole, whole] + [tile] * n + [pl.BlockSpec(memory_space=pl.ANY)] * len(before),
            out_specs=out,
        ),
        out_shape=_hbm((NY, total, chan)),
        input_output_aliases={3 + n: 0} if before else {},
        compiler_params=_params(),
        cost_estimate=_cost(2 * n * total * chan * chan, n << 19),
    )(s, blocks, blocks_other, *[own[d] for d in ds], *[other[d] for d in ds], *before)


def tail_kernel(group, wire_ref, rt_ref, tw_ref, *refs):
    parts, (out_ref, scr) = refs[:CHUNKS], refs[CHUNKS:]
    outer, inner = tw_ref.shape
    chan = out_ref.shape[2]
    rows = inner // NY // CHUNKS
    g = pl.program_id(0)

    @pl.when(g == 0)
    def _():
        for c in range(chan // 128):
            scr[c] = wire_ref[:, :, :, c * 128 : c * 128 + 128].astype(F32).reshape(scr.shape[1:])

    for k in range(group):
        a = g * group + k
        col = _column(tw_ref[pl.ds(a, 1), :], inner)
        grad = [(scr[c, pl.ds(a, inner, stride=outer), :] * col).astype(BF16) for c in range(chan // 128)]
        acc = jnp.dot(rt_ref[...], jnp.concatenate(grad, axis=1), preferred_element_type=F32)
        for q in range(NY):
            for u in range(CHUNKS):
                at = (q * CHUNKS + u) * rows
                part = parts[u][q, k * rows : k * rows + rows].astype(F32)
                out_ref[k, at : at + rows, :] = (acc[at : at + rows] + part).astype(BF16)


def tail_pass(wire, right_t, twiddle, parts):
    outer, inner = twiddle.shape
    chan = wire.shape[3]
    group = outer // 2
    part = pl.BlockSpec((NY, group * inner // NY // CHUNKS, chan), lambda g: (0, g, 0))
    return pl.pallas_call(
        functools.partial(tail_kernel, group),
        name="tail",
        grid=(outer // group,),
        in_specs=[
            pl.BlockSpec(wire.shape, lambda g: (0, 0, 0, 0)),
            pl.BlockSpec(right_t.shape, lambda g: (0, 0)),
            pl.BlockSpec(twiddle.shape, lambda g: (0, 0)),
        ]
        + [part] * CHUNKS,
        out_specs=pl.BlockSpec((group, inner, chan), lambda g: (g, 0, 0)),
        scratch_shapes=[pltpu.VMEM((chan // 128, outer * inner, 128), F32)],
        out_shape=jax.ShapeDtypeStruct((outer, inner, chan), BF16),
        compiler_params=_params(),
        cost_estimate=_cost(2 * outer * inner * inner * chan, 7 << 20),
    )(wire, right_t, twiddle, *parts)


def seq_swap(wire):
    return lax.all_to_all(wire, "seq", split_axis=0, concat_axis=0, tiled=True)


def body(inputs, twiddle, right_factor, left_factor, blocks, block_mixer, out_grad):
    outer, inner = twiddle.shape
    chan = inputs.shape[1]
    seq = left_factor.shape[0] // outer
    n = 2 * NY

    def to_pair(v):
        return lax.ppermute(v, "chan", [(c, c ^ 1) for c in range(n)])

    def around(parts):
        return [parts[0]] + [
            lax.ppermute(parts[d], "chan", [(c, (c + 2 * d) % n) for c in range(n)]) for d in range(1, NY)
        ]

    s = lax.axis_index("chan").reshape(1)
    x3 = inputs.reshape(outer, inner, chan)
    og3 = out_grad.reshape(outer, inner, chan)
    mixer = jnp.transpose(block_mixer, (1, 2, 0))

    twisted, first = right_pass(x3, right_factor, twiddle, seq)
    xp0 = to_pair(first)
    twisted = seq_swap(twisted)
    left_t = turn_pass(left_factor)
    later = pick_pass(x3, 1)
    xp1 = to_pair(later)
    middle0 = middle_pass(s, x3, xp0, blocks, 0)
    middle1 = middle_pass(s, x3, xp1, blocks, 1)
    mixed_wire = left_pass(left_factor, twisted)
    mixed = seq_swap(mixed_wire)
    blocks_other = to_pair(blocks)
    state = ()
    for u, middle in enumerate((middle0, middle1)):
        middle = around(middle)
        middle = mix_pass(s, mixer, middle, False)
        middle = around(middle)
        state = gate_pass(s, og3, middle, seq, u, state)
    gate3, grad_mixed = state[0].reshape(x3.shape), state[1].reshape(mixed_wire.shape)

    grad_mixed, mixed = lax.optimization_barrier((grad_mixed, mixed))
    grad_wire = seq_swap(grad_mixed)
    grads, others = [], []
    for u in range(CHUNKS):
        cots = cot_pass(s, mixed, og3, u)
        cots = around(cots)
        cots = mix_pass(s, mixer, cots, True)
        grads.append(around(cots))
        others.append([None] * NY)
        for d in (0, 1, 3, 2):
            others[u][d] = to_pair(grads[u][d])
    output = out_pass(mixed, gate3)
    grad_wire = left_pass(left_t, grad_wire)
    grad_twisted = seq_swap(grad_wire)
    part0 = chan_pass(s, blocks, blocks_other, grads[0], others[0], (0, 1, 3, 2), ())
    part1 = chan_pass(s, blocks, blocks_other, grads[1], others[1], (0, 1, 3), ())
    part1 = chan_pass(s, blocks, blocks_other, grads[1], others[1], (2,), (part1,))
    input_grad = tail_pass(grad_twisted, right_factor.T, twiddle, (part0, part1))
    return (output.reshape(inputs.shape), input_grad.reshape(inputs.shape))


def solution(mesh):
    return jax.shard_map(
        body,
        mesh=mesh,
        in_specs=(
            P("seq", "chan"),
            P("seq", None),
            P(),
            P(),
            P("chan", None),
            P(),
            P("seq", "chan"),
        ),
        out_specs=(P("seq", "chan"), P("seq", "chan")),
        check_vma=False,
    )
```

```python
import functools

import jax
import jax.numpy as jnp
from jax import lax
from jax.experimental import pallas as pl
from jax.experimental.pallas import tpu as pltpu
from jax.sharding import PartitionSpec as P


F32 = jnp.float32
BF16 = jnp.bfloat16
NY = 4
MIB = 24
CHUNKS = 2


def _params(mib=MIB):
    return pltpu.CompilerParams(vmem_limit_bytes=min(mib << 20, 67043328))


def in_hbm(v):
    return pltpu.with_memory_space_constraint(v, pltpu.HBM)


def _hbm(shape):
    return pltpu.HBM(shape, BF16)


def _cost(flops, nbytes):
    return pl.CostEstimate(flops=flops, bytes_accessed=nbytes, transcendentals=0)


def _fwd(s, d):
    return lax.rem(s[0] // 2 + d, NY)


def _back(s, d):
    return lax.rem(s[0] // 2 + NY - d, NY)


def _column(row, length):
    return jnp.transpose(jnp.broadcast_to(row, (128, length)))


def right_kernel(x_ref, r_ref, tw_ref, out_ref, first_ref, scr):
    outer, _, chan = x_ref.shape
    rows = r_ref.shape[0]
    part = x_ref.shape[1] // (NY * CHUNKS)
    for k in range(first_ref.shape[1] // part):
        at = pl.multiple_of(pl.program_id(0) * rows, rows) + k * part * CHUNKS
        first_ref[:, k * part : k * part + part, :] = x_ref[:, pl.ds(at, part), :]
    for a in range(outer):
        acc = jnp.dot(r_ref[...], x_ref[a], preferred_element_type=F32)
        col = _column(tw_ref[a : a + 1, :], rows)
        for c in range(chan // 128):
            scr[c, pl.ds(a, rows, stride=outer), :] = acc[:, c * 128 : c * 128 + 128] * col
    for c in range(chan // 128):
        out_ref[:, :, :, c * 128 : c * 128 + 128] = scr[c].reshape(*out_ref.shape[:3], 128).astype(BF16)


def right_pass(x3, right, twiddle, seq):
    outer, inner, chan = x3.shape
    steps = 2
    rows = inner // steps
    per = inner // seq
    return pl.pallas_call(
        right_kernel,
        name="right",
        grid=(steps,),
        in_specs=[
            pl.BlockSpec((outer, inner, chan), lambda g: (0, 0, 0)),
            pl.BlockSpec((rows, inner), lambda g: (g, 0)),
            pl.BlockSpec((outer, rows), lambda g: (0, g)),
        ],
        out_specs=[
            pl.BlockSpec((seq // steps, per, outer, chan), lambda g: (g, 0, 0, 0)),
            pl.BlockSpec((outer, rows // CHUNKS, chan), lambda g: (0, g, 0)),
        ],
        out_shape=[_hbm((seq, per, outer, chan)), _hbm((outer, inner // CHUNKS, chan))],
        scratch_shapes=[pltpu.VMEM((chan // 128, rows * outer, 128), F32)],
        compiler_params=_params(24),
        cost_estimate=_cost(2 * outer * inner * inner * chan, 6 << 20),
    )(in_hbm(x3), in_hbm(right), in_hbm(twiddle))


def left_kernel(l_ref, in_ref, out_ref):
    seq, per, outer, chan = in_ref.shape
    for j in range(per):
        block = in_ref[:, j].astype(F32).reshape(seq * outer, chan).astype(BF16)
        acc = jnp.dot(l_ref[...], block, preferred_element_type=F32)
        out_ref[:, j] = acc.reshape(seq, outer, chan).astype(BF16)


def left_pass(left, wire):
    seq, per, outer, chan = wire.shape
    steps = 2
    full = seq * outer
    block = (seq, per // steps, outer, chan)
    return pl.pallas_call(
        left_kernel,
        name="left",
        grid=(steps,),
        in_specs=[
            pl.BlockSpec((full, full), lambda g: (0, 0)),
            pl.BlockSpec(block, lambda g: (0, g, 0, 0)),
        ],
        out_specs=pl.BlockSpec(block, lambda g: (0, g, 0, 0)),
        out_shape=_hbm(wire.shape),
        compiler_params=_params(),
        cost_estimate=_cost(2 * full * full * per * chan, 4 << 20),
    )(left, wire)


def turn_kernel(in_ref, out_ref):
    out_ref[...] = jnp.transpose(in_ref[...].astype(F32)).astype(BF16)


def turn_pass(matrix):
    return pl.pallas_call(
        turn_kernel,
        name="turn",
        out_shape=_hbm(matrix.shape),
        compiler_params=_params(),
        cost_estimate=_cost(0, 1 << 18),
    )(matrix)


def pick_kernel(x_ref, out_ref):
    out_ref[...] = x_ref[...]


def pick_pass(x3, u):
    outer, inner, chan = x3.shape
    rows = inner // (NY * CHUNKS)
    x5 = x3.reshape(outer, NY, CHUNKS * rows, chan)
    out = pl.pallas_call(
        pick_kernel,
        name="pick",
        grid=(1,),
        in_specs=[pl.BlockSpec((outer, NY, rows, chan), lambda g: (0, 0, u, 0))],
        out_specs=pl.BlockSpec((outer, NY, rows, chan), lambda g: (0, 0, 0, 0)),
        out_shape=_hbm((outer, NY, rows, chan)),
        compiler_params=_params(),
        cost_estimate=_cost(0, 2 << 20),
    )(in_hbm(x5))
    return out.reshape(outer, NY * rows, chan)


def middle_kernel(s, x_ref, xp_ref, b_ref, *outs):
    outer, _, rows, chan = x_ref.shape
    half = lax.rem(s[0], 2)
    own = b_ref[:, pl.ds(pl.multiple_of(half * chan, 128), chan)]
    other = b_ref[:, pl.ds(pl.multiple_of((1 - half) * chan, 128), chan)]
    dims = (((1,), (1,)), ((), ()))
    for d in range(NY):
        q = _fwd(s, d)
        x = x_ref[:, pl.ds(q, 1)].reshape(outer * rows, chan)
        xp = xp_ref[:, pl.ds(q, 1)].reshape(outer * rows, chan)
        acc = lax.dot_general(x, own, dims, preferred_element_type=F32)
        acc += lax.dot_general(xp, other, dims, preferred_element_type=F32)
        outs[d][...] = acc.astype(BF16)


def middle_pass(s, x3, xp3, blocks, u):
    outer, inner, chan = x3.shape
    rows = inner // (NY * CHUNKS)
    block = (outer, NY, rows, chan)
    out = (outer * rows, chan)
    return pl.pallas_call(
        middle_kernel,
        name="middle",
        grid_spec=pltpu.PrefetchScalarGridSpec(
            num_scalar_prefetch=1,
            grid=(1,),
            in_specs=[
                pl.BlockSpec(block, lambda g, s: (0, 0, u, 0)),
                pl.BlockSpec(block, lambda g, s: (0, 0, 0, 0)),
                pl.BlockSpec(blocks.shape, lambda g, s: (0, 0)),
            ],
            out_specs=[pl.BlockSpec(out, lambda g, s: (0, 0))] * NY,
        ),
        out_shape=[_hbm(out)] * NY,
        compiler_params=_params(),
        cost_estimate=_cost(4 * outer * rows * NY * chan * chan, 3 << 20),
    )(s, in_hbm(x3.reshape(outer, NY, CHUNKS * rows, chan)), xp3.reshape(block), in_hbm(blocks))


def mix_kernel(flip, s, mix_ref, *refs):
    ins, outs = refs[:NY], refs[NY:]
    y = s[0] // 2
    rows = 64

    def rows_of(g, _):
        at = pl.ds(pl.multiple_of(g * rows, rows), rows)
        values = [r[at, :].astype(F32) for r in ins]
        for e in range(NY):
            to = lax.rem(y + e, NY)
            acc = None
            for d in range(NY):
                frm = lax.rem(y + NY - d, NY)
                row = mix_ref[frm, pl.ds(to, 1), :] if flip else mix_ref[to, pl.ds(frm, 1), :]
                term = values[d] * row
                acc = term if acc is None else acc + term
            outs[e][at, :] = acc.astype(BF16)
        return _

    lax.fori_loop(0, ins[0].shape[0] // rows, rows_of, 0)


def mix_pass(s, mixer, parts, flip):
    total, chan = parts[0].shape
    steps = 1
    block = pl.BlockSpec((total // steps, chan), lambda g, s: (g, 0))
    return pl.pallas_call(
        functools.partial(mix_kernel, flip),
        name="mix",
        grid_spec=pltpu.PrefetchScalarGridSpec(
            num_scalar_prefetch=1,
            grid=(steps,),
            in_specs=[pl.BlockSpec((NY, NY, chan), lambda g, s: (0, 0, lax.rem(s[0], 2)))] + [block] * NY,
            out_specs=[block] * NY,
        ),
        out_shape=[_hbm((total, chan))] * NY,
        compiler_params=_params(),
        cost_estimate=_cost(2 * NY * NY * total * chan, 2 << 20),
    )(s, in_hbm(mixer), *parts)


def gate_kernel(s, og_ref, *refs):
    pieces = refs[:NY]
    gate_ref, wire_ref, scr = refs[-3:]
    outer, _, rows, chan = og_ref.shape

    def one(a, _):
        for d in range(NY):
            q = _back(s, d)
            g = pieces[d][pl.ds(pl.multiple_of(a * rows, rows), rows), :]
            gate_ref[a, q] = g
            for c in range(chan // 128):
                cols = slice(c * 128, c * 128 + 128)
                og = og_ref[a, q, :, cols].astype(F32)
                scr[d * (chan // 128) + c, pl.ds(a, rows, stride=outer), :] = og * g[:, cols].astype(F32)
        return _

    lax.fori_loop(0, outer, one, 0)
    for d in range(NY):
        for c in range(chan // 128):
            value = scr[d * (chan // 128) + c].reshape(*wire_ref.shape[1:4], 128).astype(BF16)
            wire_ref[_back(s, d), :, :, :, c * 128 : c * 128 + 128] = value


def gate_pass(s, og3, pieces, seq, u, before):
    outer, inner, chan = og3.shape
    rows = inner // (NY * CHUNKS)
    per = inner // seq
    nat_shape = (outer, NY, CHUNKS * rows, chan)
    wire_shape = (NY, seq // NY, per, outer, chan)
    nat = pl.BlockSpec((outer, NY, rows, chan), lambda g, s: (0, 0, u, 0))
    whole = pl.BlockSpec(pieces[0].shape, lambda g, s: (0, 0))
    wire = pl.BlockSpec((NY, seq // NY // CHUNKS, per, outer, chan), lambda g, s: (0, u, 0, 0, 0))
    return pl.pallas_call(
        gate_kernel,
        name="gate",
        grid_spec=pltpu.PrefetchScalarGridSpec(
            num_scalar_prefetch=1,
            grid=(1,),
            in_specs=[nat] + [whole] * NY + [pl.BlockSpec(memory_space=pl.ANY)] * len(before),
            out_specs=[nat, wire],
            scratch_shapes=[pltpu.VMEM((NY * (chan // 128), rows * outer, 128), F32)],
        ),
        out_shape=[_hbm(nat_shape), _hbm(wire_shape)],
        input_output_aliases={2 + NY + i: i for i in range(len(before))},
        compiler_params=_params(),
        cost_estimate=_cost(outer * rows * NY * chan, 4 << 20),
    )(s, in_hbm(og3.reshape(nat_shape)), *pieces, *before)


def cot_kernel(s, wire_ref, og_ref, *refs):
    pieces, scr = refs[:NY], refs[NY]
    outer, _, rows, chan = og_ref.shape
    for d in range(NY):
        for c in range(chan // 128):
            cols = slice(c * 128, c * 128 + 128)
            value = wire_ref[_fwd(s, d), :, :, :, cols].astype(F32)
            scr[d * (chan // 128) + c] = value.reshape(scr.shape[1:])

    def one(a, _):
        at = pl.ds(pl.multiple_of(a * rows, rows), rows)
        for d in range(NY):
            for c in range(chan // 128):
                cols = slice(c * 128, c * 128 + 128)
                m = scr[d * (chan // 128) + c, pl.ds(a, rows, stride=outer), :]
                pieces[d][at, cols] = (og_ref[a, _fwd(s, d), :, cols].astype(F32) * m).astype(BF16)
        return _

    lax.fori_loop(0, outer, one, 0)


def cot_pass(s, wire, og3, u):
    outer, inner, chan = og3.shape
    seq, per = wire.shape[:2]
    rows = inner // (NY * CHUNKS)
    piece = (outer * rows, chan)
    return pl.pallas_call(
        cot_kernel,
        name="cot",
        grid_spec=pltpu.PrefetchScalarGridSpec(
            num_scalar_prefetch=1,
            grid=(1,),
            in_specs=[
                pl.BlockSpec((NY, seq // NY // CHUNKS, per, outer, chan), lambda g, s: (0, u, 0, 0, 0)),
                pl.BlockSpec((outer, NY, rows, chan), lambda g, s: (0, 0, u, 0)),
            ],
            out_specs=[pl.BlockSpec(piece, lambda g, s: (0, 0))] * NY,
            scratch_shapes=[pltpu.VMEM((NY * (chan // 128), rows * outer, 128), F32)],
        ),
        out_shape=[_hbm(piece)] * NY,
        compiler_params=_params(),
        cost_estimate=_cost(outer * rows * NY * chan, 3 << 20),
    )(s, wire.reshape(NY, seq // NY, per, outer, chan), in_hbm(og3.reshape(outer, NY, CHUNKS * rows, chan)))


def out_kernel(wire_ref, gate_ref, out_ref, scr):
    outer, rows, chan = out_ref.shape
    for c in range(chan // 128):
        scr[c] = wire_ref[:, :, :, c * 128 : c * 128 + 128].astype(F32).reshape(scr.shape[1:])
    for a in range(outer):
        for c in range(chan // 128):
            cols = slice(c * 128, c * 128 + 128)
            m = scr[c, pl.ds(a, rows, stride=outer), :]
            out_ref[a, :, cols] = (gate_ref[a, :, cols].astype(F32) * m).astype(BF16)


def out_pass(wire, gate3):
    outer, inner, chan = gate3.shape
    seq, per = wire.shape[:2]
    rows = inner // NY
    nat = pl.BlockSpec((outer, rows, chan), lambda d: (0, d, 0))
    return pl.pallas_call(
        out_kernel,
        name="out",
        grid=(NY,),
        in_specs=[pl.BlockSpec((seq // NY, per, outer, chan), lambda d: (d, 0, 0, 0)), nat],
        out_specs=nat,
        out_shape=_hbm(gate3.shape),
        scratch_shapes=[pltpu.VMEM((chan // 128, rows * outer, 128), F32)],
        compiler_params=_params(),
        cost_estimate=_cost(outer * inner * chan, 6 << 20),
    )(wire, in_hbm(gate3))


def chan_kernel(ds, s, b_ref, bo_ref, *refs):
    n = len(ds)
    own, other, out_ref = refs[:n], refs[n : 2 * n], refs[-1]
    chan = out_ref.shape[2]
    cols = pl.ds(pl.multiple_of(lax.rem(s[0], 2) * chan, 128), chan)
    for i in range(n):
        acc = jnp.dot(own[i][...], b_ref[:, cols], preferred_element_type=F32)
        acc += jnp.dot(other[i][...], bo_ref[:, cols], preferred_element_type=F32)
        out_ref[0 if n == 1 else _back(s, ds[i])] = acc.astype(BF16)


def chan_pass(s, blocks, blocks_other, own, other, ds, before):
    total, chan = own[0].shape
    whole = pl.BlockSpec(blocks.shape, lambda g, s: (0, 0))
    tile = pl.BlockSpec((total, chan), lambda g, s: (0, 0))
    if len(ds) == 1:
        out = pl.BlockSpec((1, total, chan), lambda g, s: (_back(s, ds[0]), 0, 0))
    else:
        out = pl.BlockSpec((NY, total, chan), lambda g, s: (0, 0, 0))
    n = 2 * len(ds)
    return pl.pallas_call(
        functools.partial(chan_kernel, ds),
        name="chan",
        grid_spec=pltpu.PrefetchScalarGridSpec(
            num_scalar_prefetch=1,
            grid=(1,),
            in_specs=[whole, whole] + [tile] * n + [pl.BlockSpec(memory_space=pl.ANY)] * len(before),
            out_specs=out,
        ),
        out_shape=_hbm((NY, total, chan)),
        input_output_aliases={3 + n: 0} if before else {},
        compiler_params=_params(),
        cost_estimate=_cost(2 * n * total * chan * chan, n << 19),
    )(s, in_hbm(blocks), blocks_other, *[in_hbm(own[d]) for d in ds], *[other[d] for d in ds], *before)


def tail_kernel(group, wire_ref, rt_ref, tw_ref, *refs):
    parts, (out_ref, scr) = refs[:CHUNKS], refs[CHUNKS:]
    outer, inner = tw_ref.shape
    chan = out_ref.shape[2]
    rows = inner // NY // CHUNKS
    g = pl.program_id(0)

    @pl.when(g == 0)
    def _():
        for c in range(chan // 128):
            scr[c] = wire_ref[:, :, :, c * 128 : c * 128 + 128].astype(F32).reshape(scr.shape[1:])

    for k in range(group):
        a = g * group + k
        col = _column(tw_ref[pl.ds(a, 1), :], inner)
        grad = [(scr[c, pl.ds(a, inner, stride=outer), :] * col).astype(BF16) for c in range(chan // 128)]
        acc = jnp.dot(rt_ref[...], jnp.concatenate(grad, axis=1), preferred_element_type=F32)
        for q in range(NY):
            for u in range(CHUNKS):
                at = (q * CHUNKS + u) * rows
                part = parts[u][q, k * rows : k * rows + rows].astype(F32)
                out_ref[k, at : at + rows, :] = (acc[at : at + rows] + part).astype(BF16)


def tail_pass(wire, right_t, twiddle, parts):
    outer, inner = twiddle.shape
    chan = wire.shape[3]
    group = outer // 2
    part = pl.BlockSpec((NY, group * inner // NY // CHUNKS, chan), lambda g: (0, g, 0))
    return pl.pallas_call(
        functools.partial(tail_kernel, group),
        name="tail",
        grid=(outer // group,),
        in_specs=[
            pl.BlockSpec(wire.shape, lambda g: (0, 0, 0, 0)),
            pl.BlockSpec(right_t.shape, lambda g: (0, 0)),
            pl.BlockSpec(twiddle.shape, lambda g: (0, 0)),
        ]
        + [part] * CHUNKS,
        out_specs=pl.BlockSpec((group, inner, chan), lambda g: (g, 0, 0)),
        scratch_shapes=[pltpu.VMEM((chan // 128, outer * inner, 128), F32)],
        out_shape=jax.ShapeDtypeStruct((outer, inner, chan), BF16),
        compiler_params=_params(24),
        cost_estimate=_cost(2 * outer * inner * inner * chan, 7 << 20),
    )(wire, right_t, in_hbm(twiddle), *[in_hbm(p) for p in parts])


def seq_swap(wire):
    return lax.all_to_all(wire, "seq", split_axis=0, concat_axis=0, tiled=True)


def body(inputs, twiddle, right_factor, left_factor, blocks, block_mixer, out_grad):
    outer, inner = twiddle.shape
    chan = inputs.shape[1]
    seq = left_factor.shape[0] // outer
    n = 2 * NY

    def to_pair(v):
        return lax.ppermute(v, "chan", [(c, c ^ 1) for c in range(n)])

    def around(parts):
        return [in_hbm(parts[0])] + [
            lax.ppermute(parts[d], "chan", [(c, (c + 2 * d) % n) for c in range(n)]) for d in range(1, NY)
        ]

    s = lax.axis_index("chan").reshape(1)
    x3 = inputs.reshape(outer, inner, chan)
    og3 = out_grad.reshape(outer, inner, chan)
    mixer = jnp.transpose(block_mixer, (1, 2, 0))

    twisted, first = right_pass(x3, right_factor, twiddle, seq)
    xp0 = to_pair(first)
    twisted = seq_swap(twisted)
    left_t = turn_pass(left_factor)
    right_t = turn_pass(right_factor)
    later = pick_pass(x3, 1)
    xp1 = to_pair(later)
    middle0 = middle_pass(s, x3, xp0, blocks, 0)
    middle1 = middle_pass(s, x3, xp1, blocks, 1)
    mixed_wire = left_pass(left_factor, twisted)
    mixed = seq_swap(mixed_wire)
    blocks_other = to_pair(blocks)
    state = ()
    for u, middle in enumerate((middle0, middle1)):
        middle = around(middle)
        middle = mix_pass(s, mixer, middle, False)
        middle = around(middle)
        state = gate_pass(s, og3, middle, seq, u, state)
    gate3, grad_mixed = state[0].reshape(x3.shape), state[1].reshape(mixed_wire.shape)

    grad_mixed, mixed = lax.optimization_barrier((grad_mixed, mixed))
    grad_wire = seq_swap(grad_mixed)
    grads, others = [], []
    for u in range(CHUNKS):
        cots = cot_pass(s, mixed, og3, u)
        cots = around(cots)
        cots = mix_pass(s, mixer, cots, True)
        grads.append(around(cots))
        others.append([None] * NY)
        for d in (0, 1, 3, 2):
            others[u][d] = to_pair(grads[u][d])
    output = out_pass(mixed, gate3)
    grad_wire = left_pass(left_t, grad_wire)
    grad_twisted = seq_swap(grad_wire)
    part0 = chan_pass(s, blocks, blocks_other, grads[0], others[0], (0, 1, 3, 2), ())
    part1 = chan_pass(s, blocks, blocks_other, grads[1], others[1], (0, 1, 3), ())
    part1 = chan_pass(s, blocks, blocks_other, grads[1], others[1], (2,), (part1,))
    input_grad = tail_pass(grad_twisted, right_t, twiddle, (part0, part1))
    return (output.reshape(inputs.shape), input_grad.reshape(inputs.shape))


def solution(mesh):
    return jax.shard_map(
        body,
        mesh=mesh,
        in_specs=(
            P("seq", "chan"),
            P("seq", None),
            P(),
            P(),
            P("chan", None),
            P(),
            P("seq", "chan"),
        ),
        out_specs=(P("seq", "chan"), P("seq", "chan")),
        check_vma=False,
    )
```
